32 devices in a mesh: frame: 8 (over y, x, core), tile: 4 (over z).
Axes of the slice: x: 2, y: 2, z: 4, core: 2. Of those that a mesh axis runs over, the one named last changes fastest.
Arguments:
- features: bfloat16 [8, 32, 4096], P('frame', None, 'tile'), may hold values from -6 to 6
- views: int32 [8, 4], replicated, may hold values from 0 to 7, as said below
- offsets: int32 [8, 4, 32, 32], P('frame', None, None, 'tile'), may hold values from -2 to 2
- kernels: bfloat16 [32, 128, 128], replicated, may hold values from -0.5 to 0.5
- reg_weight: bfloat16 [3, 8, 32], replicated, may hold values from -0.625 to 0.625
- head_weight: float32 [8], replicated, may hold values from -2 to 2
- depth_cot: float32 [8, 4096], P('frame', 'tile'), may hold values from -120 to 120
Outputs:
- depth: float32 [8, 4096], P('frame', 'tile')
- feature_grad: float32 [8, 32, 4096], P('frame', None, 'tile')
The draws below stay inside these ranges and needn't reach their ends.
Inputs may be any that keep to these rules, and one draw needn't show every extreme that they name: `views`: row f lists 4 different frames, none of them f.
All inputs are finite; a program needn't handle non-finite values.
Results may differ from the reference program's by a relative error of at most 0.017.
The reference program's roundings to bfloat16 on the way count: a program that leaves them out, or rounds other values in their place, can miss the bound.
Values may be sent and summed in bfloat16 or wider, within the bound.
No kernel may reach another device: no remote copies, remote signals or barrier semaphores. Data moves between devices by JAX's collectives and lax.ppermute only.
A program may use at most 64 MiB of HBM per device.

```python
import jax
import jax.numpy as jnp
from jax import lax

C = 32
P_SIZE = 32
R = 8
V = 4
HB = 2
F = 8
NBLK = 32
PIX = 4096


def draw_views(key, part):
    scores = jax.random.randint(key, (F, F - 1), 0, 1 << 20)
    columns = jnp.arange(F - 1, dtype=jnp.int32)[None, :]
    frame_rows = jnp.arange(F, dtype=jnp.int32)[:, None]
    scores = scores * F + columns
    forced = (frame_rows == 0) & (columns == F - 2) | (frame_rows == F - 1) & (columns == 0)
    scores = jnp.where(forced, (1 << 20) * F + F, scores)
    chosen = lax.top_k(scores, V)[1]
    return ((frame_rows + 1 + chosen) % F).astype(jnp.int32)


def with_ends(values, key, least, high):
    spot = [jax.random.randint(jax.random.fold_in(key, axis), (), 0, length) for axis, length in enumerate(values.shape)]
    longest = values.shape.index(max(values.shape))
    next_to = spot[:longest] + [(spot[longest] + 1) % values.shape[longest]] + spot[longest + 1:]
    return values.at[tuple(spot)].set(least).at[tuple(next_to)].set(high)


def block_scale(stream_key, shape, pieces, smallest, top_value):
    level = 1.0
    for position, shards_of in pieces:
        steps = jax.random.uniform(jax.random.fold_in(jax.random.fold_in(stream_key, 6), position), (shards_of,), jnp.float32, smallest / len(pieces), top_value / len(pieces))
        level = level * jnp.repeat(jnp.exp(steps), shape[position] // shards_of).reshape((-1,) + (1,) * (len(shape) - 1 - position))
    return level


def noise(stream_key, shape, scale, most, shards=(), kind=jnp.bfloat16):
    values = scale * jax.random.normal(stream_key, shape, jnp.float32)
    if shards:
        values = values * block_scale(stream_key, shape, shards, -0.22, 0.18)
    return jnp.clip(values, -most, most).astype(kind)


def setup_inputs(seed: int = 0) -> dict:
    key_of = jax.random.split(jax.random.key(seed), 8)
    return {
        "features": noise(key_of[0], (F, C, PIX), 1.0, 6.0, ((0, 8), (2, 4))),
        "views": draw_views(jax.random.fold_in(key_of[7], 71), 0),
        "offsets": with_ends(jax.random.randint(key_of[2], (F, V, P_SIZE, NBLK), -HB, HB + 1), jax.random.fold_in(key_of[2], 1), -HB, HB).astype(jnp.int32),
        "kernels": noise(key_of[3], (P_SIZE, 128, 128), 128 ** -0.5, 0.5),
        "reg_weight": noise(key_of[4], (3, R, C), (3 * C) ** -0.5, 0.625),
        "head_weight": noise(key_of[5], (R,), R ** -0.5, 2.0, (), jnp.float32),
        "depth_cot": noise(key_of[6], (F, PIX), 20.0, 120.0, ((0, 8), (1, 4)), jnp.float32),
    }


def warp_plane(reference_feat, sources, shifts, kernel):
    vcount, channels, pixels = sources.shape
    block_count = pixels // 128
    blocks = sources.reshape(vcount, channels, block_count, 128)
    target = jnp.arange(block_count, dtype=jnp.int32)[None, :] + shifts
    inside = (target >= 0) & (target < block_count)
    clipped = jnp.clip(target, 0, block_count - 1).astype(jnp.int32)
    picked = jax.vmap(lambda blockset, where_at: jnp.take(blockset, where_at, axis=1))(blocks, clipped)
    picked = jnp.where(inside[:, None, :, None], picked, 0.0).astype(jnp.bfloat16)
    warped = jnp.dot(picked.reshape(-1, 128), kernel, preferred_element_type=jnp.float32)
    warped = warped.reshape(vcount, channels, pixels)
    stacked = jnp.concatenate([reference_feat[None], warped], axis=0)
    average = lax.optimization_barrier(jnp.sum(stacked, axis=0)) / (V + 1)
    centred = stacked - average[None]
    return (lax.optimization_barrier(jnp.sum(centred * centred, axis=0)) / (V + 1)).astype(jnp.bfloat16)

def regularize(volume, reg_weight, head_weight):
    planes = volume.astype(jnp.float32)
    padded = jnp.pad(planes, ((1, 1), (0, 0), (0, 0)))
    hidden = jnp.einsum('rc,dcp->drp', reg_weight[0].astype(jnp.float32), padded[0:P_SIZE])
    for tap_index in range(1, 3):
        hidden = hidden + jnp.einsum('rc,dcp->drp', reg_weight[tap_index].astype(jnp.float32), padded[tap_index:tap_index + P_SIZE])
    scores = 4.0 * jnp.tanh(lax.optimization_barrier(jnp.sum(hidden * head_weight[None, :, None], axis=1)))
    weights = jnp.exp(scores)
    values = (jnp.arange(P_SIZE, dtype=jnp.float32) + 1.0) / P_SIZE
    return lax.optimization_barrier(jnp.sum(weights * values[:, None], axis=0)) / lax.optimization_barrier(jnp.sum(weights, axis=0))

def reference(features, views, offsets, kernels, reg_weight, head_weight, depth_cot):

    def all_depth(feat_copy):

        def one_frame(frame_id):
            reference_feat = feat_copy[frame_id]
            sources = feat_copy[views[frame_id]]
            shifts = jnp.transpose(offsets[frame_id], (1, 0, 2))

            def per_plane(plane_items):
                return warp_plane(reference_feat, sources, plane_items[0], plane_items[1])
            volume = lax.map(jax.checkpoint(per_plane), (shifts, kernels))
            return regularize(volume, reg_weight, head_weight)
        return lax.map(jax.checkpoint(one_frame), jnp.arange(F, dtype=jnp.int32))
    feat_copy = features.astype(jnp.float32)
    depth_map, pullback = jax.vjp(all_depth, feat_copy)
    feature_grad = pullback(depth_cot)[0]
    return (depth_map, feature_grad)
```

```python
import functools

import jax
import jax.numpy as jnp
from jax import lax
from jax.experimental import pallas as pl
from jax.experimental.pallas import tpu as pltpu
from jax.sharding import PartitionSpec as P

V = 4
HB = 2
BLK = 128
F32 = jnp.float32
BF16 = jnp.bfloat16


def depth_kernel(
    views, offsets, head, feat, gathered, rim_left, rim_right, kernels, reg, cot,
    depth, ref_grad, core_grad, grad_left, grad_right,
    src, centred, partial, dscore, taps, *grads,
):
    frame_count, channels, pixels = gathered.shape
    nblk = pixels // BLK
    planes = kernels.shape[0]
    tap_count, hidden_count = reg.shape[0], reg.shape[1]
    rim = HB * BLK
    views_n = V
    me = lax.axis_index("frame")

    for j in range(views_n):
        owner = views[me, j]
        for q in range(HB):
            src[j, q] = rim_left[owner, :, q * BLK : (q + 1) * BLK]
            src[j, HB + nblk + q] = rim_right[owner, :, q * BLK : (q + 1) * BLK]
        for q in range(nblk):
            src[j, HB + q] = gathered[owner, :, q * BLK : (q + 1) * BLK]
        grads[j][...] = jnp.zeros_like(grads[j])

    taps[...] = jnp.zeros_like(taps)
    for t in range(tap_count):
        row = head[0] * reg[t, 0:1, :].astype(F32)
        for r in range(1, hidden_count):
            row = row + head[r] * reg[t, r : r + 1, :].astype(F32)
        taps[0, t : t + 1, 0:channels] = row
    taps[1] = taps[0].T
    for t in range(tap_count):
        taps[2 + t, 0:channels, :] = jnp.broadcast_to(
            taps[1, 0:channels, t : t + 1], (channels, BLK)
        )

    partial[...] = jnp.zeros_like(partial)
    ref_grad[...] = jnp.zeros_like(ref_grad)
    dscore[0] = jnp.zeros_like(dscore[0])
    dscore[planes + 1] = jnp.zeros_like(dscore[planes + 1])

    def rows_of(b, j):
        start = (b * views_n + j) * channels
        return slice(start, start + channels)

    def forward(d, carry):
        picked = []
        for b in range(nblk):
            for j in range(views_n):
                picked.append(src[j, offsets[0, j, d, b] + (b + HB)])
        warped = jnp.dot(
            jnp.concatenate(picked, axis=0), kernels[d], preferred_element_type=F32
        )
        for b in range(nblk):
            lanes = slice(b * BLK, (b + 1) * BLK)
            xs = [feat[0, :, lanes].astype(F32)]
            xs += [warped[rows_of(b, j)] for j in range(views_n)]
            average = sum(xs[1:], xs[0]) * (1.0 / (views_n + 1))
            cs = [x - average for x in xs]
            for i, c in enumerate(cs):
                centred[d, i, :, lanes] = c
            total = cs[0] * cs[0]
            for c in cs[1:]:
                total = total + c * c
            variance = (total * (1.0 / (views_n + 1))).astype(BF16).astype(F32)
            for t in range(tap_count):
                product = variance * taps[2 + t, 0:channels, :]
                folded = product.reshape(channels // 8, 8, BLK).sum(axis=0)
                partial[d + 2 - t, :, lanes] += folded
        return carry

    lax.fori_loop(0, planes, forward, 0)

    values = (
        lax.broadcasted_iota(jnp.int32, (planes, BLK), 0).astype(F32) + 1.0
    ) / planes
    for b in range(nblk):
        lanes = slice(b * BLK, (b + 1) * BLK)
        raw = partial[1 : planes + 1, :, lanes].sum(axis=1)
        tanh = jnp.tanh(raw)
        weights = jnp.exp(4.0 * tanh)
        norm = jnp.sum(weights, axis=0, keepdims=True)
        result = jnp.sum(weights * values, axis=0, keepdims=True) / norm
        depth[0:1, lanes] = result
        slope = (cot[0:1, lanes] / norm) * (values - result) * weights
        draw = slope * (4.0 * (1.0 - tanh * tanh))
        for d in range(planes):
            dscore[d + 1, :, lanes] = draw[d : d + 1]

    def backward(d, carry):
        rows = []
        for b in range(nblk):
            lanes = slice(b * BLK, (b + 1) * BLK)
            dvar = jnp.zeros((channels, BLK), F32)
            for t in range(tap_count):
                dvar = dvar + taps[2 + t, 0:channels, :] * dscore[d + 2 - t, :, lanes]
            scale = dvar.astype(BF16).astype(F32) * (2.0 / (views_n + 1))
            cs = [centred[d, i, :, lanes] for i in range(views_n + 1)]
            mean = sum(cs[1:], cs[0]) * (1.0 / (views_n + 1))
            ref_grad[:, lanes] += scale * (cs[0] - mean)
            for c in cs[1:]:
                rows.append((scale * (c - mean)).astype(BF16))
        dpicked = lax.dot_general(
            jnp.concatenate(rows, axis=0), kernels[d],
            (((1,), (1,)), ((), ())), preferred_element_type=F32,
        )
        for b in range(nblk):
            for j in range(views_n):
                grads[j][offsets[0, j, d, b] + (b + HB)] += dpicked[rows_of(b, j)]
        return carry

    lax.fori_loop(0, planes, backward, 0)

    for f in range(frame_count):
        core_grad[f] = jnp.zeros_like(core_grad[f])
    for j in range(views_n):
        owner = views[me, j]
        for q in range(nblk):
            core_grad[owner, :, q * BLK : (q + 1) * BLK] = grads[j][HB + q].astype(BF16)
        for q in range(HB):
            grad_left[j, :, q * BLK : (q + 1) * BLK] = grads[j][q].astype(BF16)
            grad_right[j, :, q * BLK : (q + 1) * BLK] = grads[j][HB + nblk + q].astype(BF16)


def merge_kernel(views, from_left, from_right, core, out):
    me = lax.axis_index("frame")
    rim = HB * BLK
    out[...] = core[...]
    pixels = core.shape[2]
    for j in range(V):
        owner = views[me, j]
        out[owner, :, 0:rim] = (
            out[owner, :, 0:rim].astype(F32) + from_left[j].astype(F32)
        ).astype(BF16)
        out[owner, :, pixels - rim :] = (
            out[owner, :, pixels - rim :].astype(F32) + from_right[j].astype(F32)
        ).astype(BF16)


def per_device(features, views, offsets, kernels, reg_weight, head_weight, depth_cot):
    local_frames, channels, pixels = features.shape
    assert local_frames == 1
    frame_count = lax.axis_size("frame")
    tile_count = lax.axis_size("tile")
    rim = HB * BLK
    nblk = pixels // BLK
    planes = kernels.shape[0]
    to_next = [(i, i + 1) for i in range(tile_count - 1)]
    to_prev = [(i + 1, i) for i in range(tile_count - 1)]

    gathered = lax.all_gather(features, "frame", axis=0, tiled=True)
    rim_left = lax.ppermute(gathered[:, :, pixels - rim :], "tile", to_next)
    rim_right = lax.ppermute(gathered[:, :, :rim], "tile", to_prev)

    smem = pl.BlockSpec(memory_space=pltpu.SMEM)
    vmem = pl.BlockSpec(memory_space=pltpu.VMEM)
    depth, ref_grad, core_grad, grad_left, grad_right = pl.pallas_call(
        depth_kernel,
        out_shape=(
            jax.ShapeDtypeStruct((1, pixels), F32),
            jax.ShapeDtypeStruct((channels, pixels), F32),
            jax.ShapeDtypeStruct((frame_count, channels, pixels), BF16),
            jax.ShapeDtypeStruct((V, channels, rim), BF16),
            jax.ShapeDtypeStruct((V, channels, rim), BF16),
        ),
        in_specs=[smem, smem, smem] + [vmem] * 7,
        out_specs=(vmem,) * 5,
        scratch_shapes=[
            pltpu.VMEM((V, nblk + 2 * HB, channels, BLK), BF16),
            pltpu.VMEM((planes, V + 1, channels, pixels), F32),
            pltpu.VMEM((planes + 2, 8, pixels), F32),
            pltpu.VMEM((planes + 2, 1, pixels), F32),
            pltpu.VMEM((5, BLK, BLK), F32),
        ]
        + [pltpu.VMEM((nblk + 2 * HB, channels, BLK), F32)] * V,
        compiler_params=pltpu.CompilerParams(vmem_limit_bytes=48 << 20),
        cost_estimate=pl.CostEstimate(
            flops=4 * planes * V * channels * pixels * BLK, bytes_accessed=4 << 20,
            transcendentals=2 * planes * pixels,
        ),
        name="depth_window",
    )(
        views, offsets, head_weight, features, gathered, rim_left, rim_right, kernels,
        reg_weight, depth_cot,
    )

    from_left = lax.ppermute(grad_right, "tile", to_next)
    from_right = lax.ppermute(grad_left, "tile", to_prev)
    merged = pl.pallas_call(
        merge_kernel,
        out_shape=jax.ShapeDtypeStruct((frame_count, channels, pixels), BF16),
        in_specs=[smem] + [vmem] * 3,
        out_specs=vmem,
        name="merge_rims",
    )(views, from_left, from_right, core_grad)
    pieces = lax.all_to_all(merged, "frame", 0, 0, tiled=True)
    grad = jnp.sum(pieces.astype(F32), axis=0) + ref_grad
    return depth, grad[None]


def solution(mesh):
    return jax.shard_map(
        per_device,
        mesh=mesh,
        in_specs=(
            P("frame", None, "tile"),
            P(),
            P("frame", None, None, "tile"),
            P(),
            P(),
            P(),
            P("frame", "tile"),
        ),
        out_specs=(P("frame", "tile"), P("frame", None, "tile")),
        check_vma=False,
    )
```

```python
import jax
import jax.numpy as jnp
from jax import lax
from jax.experimental import pallas as pl
from jax.experimental.pallas import tpu as pltpu
from jax.sharding import PartitionSpec as P

V = 4
HB = 2
BLK = 128
CHUNKS = 4
BWD = 8
F32 = jnp.float32
BF16 = jnp.bfloat16
VMEM = pl.BlockSpec(memory_space=pltpu.VMEM)
SMEM = pl.BlockSpec(memory_space=pltpu.SMEM)
SMALL = pltpu.CompilerParams(vmem_limit_bytes=4 << 20)


def split3(w):
    high = w.astype(BF16).astype(F32)
    mid = (w - high).astype(BF16).astype(F32)
    return high, mid, w - high - mid


def weights_kernel(head, reg, band, band_t, rows):
    tap_count, hidden_count, channels = reg.shape
    planes = band.shape[0]
    rows[...] = jnp.zeros_like(rows)
    for t in range(tap_count):
        row = head[0] * reg[t, 0:1, :].astype(F32)
        for r in range(1, hidden_count):
            row = row + head[r] * reg[t, r : r + 1, :].astype(F32)
        rows[t : t + 1, 0:channels] = row
    columns = rows[...].T
    lane = lax.broadcasted_iota(jnp.int32, (channels, BLK), 1)
    part = lane // planes
    score = lane % planes
    weights = []
    for t in range(tap_count):
        high, mid, low = split3(
            jnp.broadcast_to(columns[0:channels, t : t + 1], (channels, BLK))
        )
        weights.append(jnp.where(part < 2, high, jnp.where(part == 2, mid, low)))
    for d in range(planes):
        tile = jnp.zeros((channels, BLK), F32)
        for t in range(tap_count):
            tile = jnp.where(score == d - t + 1, weights[t], tile)
        band[d] = tile.astype(BF16)
    per_tile = BLK // channels
    for k in range(planes // per_tile):
        tile = band[k * per_tile : (k + 1) * per_tile].reshape(BLK, BLK)
        band_t[:, k * BLK : (k + 1) * BLK] = tile.astype(F32).T.astype(BF16)


def pick_kernel(views, *refs):
    count = len(refs) - 3
    pieces, (core, first, second) = refs[:count], refs[count:]
    nblk = core.shape[1]
    me = lax.axis_index("frame")
    even = lax.axis_index("tile") % 2 == 0
    for j in range(V):
        slot = views[j, me] ^ me
        for r in range(count):

            @pl.when(slot == r + 1)
            def _(r=r, j=j):
                for q in range(nblk):
                    core[j, q] = pieces[r][0, :, q * BLK : (q + 1) * BLK]

    right, left = slice(nblk - HB, nblk), slice(0, HB)

    @pl.when(even)
    def _():
        first[...] = core[:, right]
        second[...] = core[:, left]

    @pl.when(jnp.logical_not(even))
    def _():
        first[...] = core[:, left]
        second[...] = core[:, right]


def depth_kernel(
    offsets, feat, core, first, second, kernels, band, band_t, cot,
    depth, ref_grad, core_grad, grad_first, grad_second,
    src, base, shifted, means, volume, matrices, arrived, *grads,
):
    channels, pixels = ref_grad.shape
    nblk = pixels // BLK
    planes = kernels.shape[0]
    share = 1.0 / (V + 1)
    chunk = planes // CHUNKS

    def load(k):
        part = pl.ds(k * chunk, chunk)
        return pltpu.make_async_copy(kernels.at[part], matrices.at[part], arrived.at[k])

    for k in range(CHUNKS):
        load(k).start()

    even = lax.axis_index("tile") % 2 == 0
    left, right = slice(0, HB), slice(HB + nblk, None)

    @pl.when(even)
    def _():
        src[:, right] = first[...]
        src[:, left] = second[...]

    @pl.when(jnp.logical_not(even))
    def _():
        src[:, left] = first[...]
        src[:, right] = second[...]

    for j in range(V):
        for q in range(nblk):
            src[j, HB + q] = core[j, q]
        grads[j][...] = jnp.zeros_like(grads[j])
    ref_grad[...] = jnp.zeros_like(ref_grad)
    base[...] = feat[0].astype(F32)

    def rows_of(b, j):
        start = (b * V + j) * channels
        return slice(start, start + channels)

    def forward(d, carry):
        picked = []
        for b in range(nblk):
            for j in range(V):
                picked.append(src[j, offsets[0, j, b, d] + (b + HB)])
        warped = jnp.dot(
            jnp.concatenate(picked, axis=0), matrices[d], preferred_element_type=F32
        )
        for b in range(nblk):
            lanes = slice(b * BLK, (b + 1) * BLK)
            first = base[:, lanes]
            ys = [warped[rows_of(b, j)] - first for j in range(V)]
            for j in range(V):
                shifted[d, j, :, lanes] = ys[j]
            total = (ys[0] + ys[1]) + (ys[2] + ys[3])
            mean = total * share
            squares = (ys[0] * ys[0] + ys[1] * ys[1]) + (ys[2] * ys[2] + ys[3] * ys[3])
            variance = (squares - total * mean) * share
            volume[d, :, lanes] = variance.astype(BF16)
            means[d, :, lanes] = mean + (total - (V + 1) * mean) * share
        return carry

    def forward_chunk(k, carry):
        load(k).wait()
        for i in range(chunk):
            forward(k * chunk + i, carry)
        return carry

    lax.fori_loop(0, CHUNKS, forward_chunk, 0)

    wide = BLK * (2 if nblk % 2 == 0 else 1)
    groups = [slice(i, i + wide) for i in range(0, pixels, wide)]
    values = (
        lax.broadcasted_iota(jnp.int32, (planes, wide), 0).astype(F32) + 1.0
    ) / planes
    raws = []
    for lanes in groups:
        parts = jnp.dot(
            band_t[...], volume[:, :, lanes].reshape(planes * channels, wide),
            preferred_element_type=F32,
        )
        raws.append(
            parts[0:planes]
            + (parts[2 * planes : 3 * planes] + parts[3 * planes : 4 * planes])
        )
    stacks = []
    for lanes, raw in zip(groups, raws):
        tanh = jnp.tanh(raw)
        weights = jnp.exp(4.0 * tanh)
        norm = jnp.sum(weights, axis=0, keepdims=True)
        result = jnp.sum(weights * values, axis=0, keepdims=True) / norm
        depth[0:1, lanes] = result
        slope = (cot[0:1, lanes] / norm) * (values - result) * weights
        draw = slope * (4.0 * (1.0 - tanh * tanh))
        high = draw.astype(BF16)
        low = (draw - high.astype(F32)).astype(BF16)
        stacks.append(jnp.concatenate([high, low, high, high], axis=0))
    for lanes, stack in zip(groups, stacks):
        dvolume = jnp.dot(
            band[...].reshape(planes * channels, BLK), stack, preferred_element_type=F32
        )
        volume[:, :, lanes] = dvolume.astype(BF16).reshape(planes, channels, wide)

    def backward(d, carry):
        rows = []
        for b in range(nblk):
            lanes = slice(b * BLK, (b + 1) * BLK)
            dvar = volume[d, :, lanes].astype(F32)
            mean = means[d, :, lanes]
            ref_grad[:, lanes] -= dvar * mean
            for j in range(V):
                rows.append((dvar * (shifted[d, j, :, lanes] - mean)).astype(BF16))
        dpicked = lax.dot_general(
            jnp.concatenate(rows, axis=0), matrices[d],
            (((1,), (1,)), ((), ())), preferred_element_type=F32,
        )
        for b in range(nblk):
            for j in range(V):
                grads[j][offsets[0, j, b, d] + (b + HB)] += dpicked[rows_of(b, j)]
        return carry

    lax.fori_loop(0, planes, backward, 0, unroll=BWD)

    scale = 2.0 * share
    ref_grad[...] = ref_grad[...] * scale
    for j in range(V):
        core_grad[j] = grads[j][HB : HB + nblk] * scale

    @pl.when(even)
    def _():
        for j in range(V):
            grad_first[j] = (grads[j][right] * scale).astype(BF16)
            grad_second[j] = (grads[j][left] * scale).astype(BF16)

    @pl.when(jnp.logical_not(even))
    def _():
        for j in range(V):
            grad_first[j] = (grads[j][left] * scale).astype(BF16)
            grad_second[j] = (grads[j][right] * scale).astype(BF16)


def merge_kernel(views, core, first, second, near, far, left, right):
    me = lax.axis_index("frame")
    nblk = core.shape[1]
    near[...] = jnp.zeros_like(near)
    far[...] = jnp.zeros_like(far)
    even = lax.axis_index("tile") % 2 == 0

    @pl.when(even)
    def _():
        right[...] = first[...].astype(F32)
        left[...] = second[...].astype(F32)

    @pl.when(jnp.logical_not(even))
    def _():
        left[...] = first[...].astype(F32)
        right[...] = second[...].astype(F32)

    def put(out, j, index):
        for q in range(nblk):
            tile = core[j, q]
            if q < HB:
                tile = tile + left[j, q]
            if q >= nblk - HB:
                tile = tile + right[j, q - (nblk - HB)]
            out[index, :, q * BLK : (q + 1) * BLK] = tile.astype(BF16)

    for j in range(V):
        slot = views[j, me] ^ me

        @pl.when(slot % 2 == 0)
        def _(j=j, slot=slot):
            put(near, j, slot // 2)

        @pl.when(slot % 2 == 1)
        def _(j=j, slot=slot):
            put(far, j, slot // 2)


def pair_kernel(near, received, own, *sent):
    own[...] = near[0].astype(F32) + received[0].astype(F32)
    for i, out in enumerate(sent):
        out[0] = (near[i + 1].astype(F32) + received[i + 1].astype(F32)).astype(BF16)


def exchange(x, distance):
    count = lax.axis_size("frame")
    return lax.ppermute(x, "frame", [(i, i ^ distance) for i in range(count)])


def swap_rims(first, second):
    count = lax.axis_size("tile")
    received = []
    for start, rim in ((0, first), (1, second)):
        pairs = [(i, i + 1) for i in range(start, count - 1, 2)]
        received.append(lax.ppermute(rim, "tile", pairs + [(b, a) for a, b in pairs]))
    return received


def per_device(features, views, offsets, kernels, reg_weight, head_weight, depth_cot):
    local_frames, channels, pixels = features.shape
    frame_count = lax.axis_size("frame")
    assert local_frames == 1 and frame_count & (frame_count - 1) == 0
    nblk = pixels // BLK
    planes = kernels.shape[0]
    shape = jax.ShapeDtypeStruct
    rim_shape = shape((V, HB, channels, BLK), BF16)
    views = views.T
    offsets = jnp.swapaxes(offsets, 2, 3)

    band, band_t = pl.pallas_call(
        weights_kernel,
        out_shape=(
            shape((planes, channels, BLK), BF16), shape((BLK, planes * channels), BF16),
        ),
        in_specs=[SMEM, VMEM],
        out_specs=(VMEM, VMEM),
        scratch_shapes=[pltpu.VMEM((BLK, BLK), F32)],
        compiler_params=SMALL,
        name="band_weights",
    )(head_weight, reg_weight)

    pieces = {0: features}
    for r in range(2, frame_count, 2):
        pieces[r] = exchange(features, r)
    for r in range(0, frame_count, 2):
        pieces[r + 1] = exchange(pieces[r], 1)
    core, first, second = pl.pallas_call(
        pick_kernel,
        out_shape=(shape((V, nblk, channels, BLK), BF16), rim_shape, rim_shape),
        in_specs=[SMEM] + [VMEM] * (frame_count - 1),
        out_specs=(VMEM,) * 3,
        compiler_params=SMALL,
        name="pick_views",
    )(views, *[pieces[r] for r in range(1, frame_count)])
    first, second = swap_rims(first, second)

    depth, ref_grad, core_grad, grad_first, grad_second = pl.pallas_call(
        depth_kernel,
        out_shape=(
            shape((1, pixels), F32), shape((channels, pixels), F32),
            shape((V, nblk, channels, BLK), F32), rim_shape, rim_shape,
        ),
        in_specs=[SMEM] + [VMEM] * 4 + [pl.BlockSpec(memory_space=pltpu.HBM)] + [VMEM] * 3,
        out_specs=(VMEM,) * 5,
        scratch_shapes=[
            pltpu.VMEM((V, nblk + 2 * HB, channels, BLK), BF16),
            pltpu.VMEM((channels, pixels), F32),
            pltpu.VMEM((planes, V, channels, pixels), F32),
            pltpu.VMEM((planes, channels, pixels), F32),
            pltpu.VMEM((planes, channels, pixels), BF16),
            pltpu.VMEM((planes, BLK, BLK), BF16),
            pltpu.SemaphoreType.DMA((CHUNKS,)),
        ]
        + [pltpu.VMEM((nblk + 2 * HB, channels, BLK), F32)] * V,
        compiler_params=pltpu.CompilerParams(vmem_limit_bytes=30 << 20),
        cost_estimate=pl.CostEstimate(
            flops=4 * planes * V * channels * pixels * BLK, bytes_accessed=4 << 20,
            transcendentals=2 * planes * pixels,
        ),
        name="depth_window",
    )(offsets, features, core, first, second, pltpu.with_memory_space_constraint(kernels, pltpu.HBM), band, band_t, depth_cot)

    grad_first, grad_second = swap_rims(grad_first, grad_second)
    half = shape((frame_count // 2, channels, pixels), BF16)
    near, far = pl.pallas_call(
        merge_kernel,
        out_shape=(half, half),
        in_specs=[SMEM] + [VMEM] * 3,
        out_specs=(VMEM, VMEM),
        scratch_shapes=[pltpu.VMEM((V, HB, channels, BLK), F32)] * 2,
        compiler_params=SMALL,
        name="merge_rims",
    )(views, core_grad, grad_first, grad_second)
    received = exchange(far, 1)
    own, *sent = pl.pallas_call(
        pair_kernel,
        out_shape=(shape((channels, pixels), F32),)
        + (shape((1, channels, pixels), BF16),) * (frame_count // 2 - 1),
        in_specs=[VMEM, VMEM],
        out_specs=(VMEM,) * (frame_count // 2),
        compiler_params=SMALL,
        name="add_pair",
    )(near, received)
    total = (own + ref_grad)[None]
    for i, piece in enumerate(sent):
        total = total + exchange(piece, 2 * i + 2).astype(F32)
    return depth, total


def solution(mesh):
    return jax.shard_map(
        per_device,
        mesh=mesh,
        in_specs=(
            P("frame", None, "tile"),
            P(),
            P("frame", None, None, "tile"),
            P(),
            P(),
            P(),
            P("frame", "tile"),
        ),
        out_specs=(P("frame", "tile"), P("frame", None, "tile")),
        check_vma=False,
    )
```

```python
import jax
import jax.numpy as jnp
from jax import lax
from jax.experimental import pallas as pl
from jax.experimental.pallas import tpu as pltpu
from jax.sharding import PartitionSpec as P


V = 4
HB = 2
BLK = 128
CHUNKS = 4
UNROLL = 8
F32 = jnp.float32
BF16 = jnp.bfloat16
VMEM = pl.BlockSpec(memory_space=pltpu.VMEM)
SMEM = pl.BlockSpec(memory_space=pltpu.SMEM)
SMALL = pltpu.CompilerParams(vmem_limit_bytes=4 << 20)


def split3(w):
    high = w.astype(BF16).astype(F32)
    mid = (w - high).astype(BF16).astype(F32)
    return high, mid, w - high - mid


def weights_kernel(head, reg, band, band_t, rows):
    tap_count, hidden_count, channels = reg.shape
    planes = band.shape[0]
    rows[...] = jnp.zeros_like(rows)
    for t in range(tap_count):
        row = head[0] * reg[t, 0:1, :].astype(F32)
        for r in range(1, hidden_count):
            row = row + head[r] * reg[t, r : r + 1, :].astype(F32)
        rows[t : t + 1, 0:channels] = row
    columns = rows[...].T
    lane = lax.broadcasted_iota(jnp.int32, (channels, BLK), 1)
    part = lane // planes
    score = lane % planes
    weights = []
    for t in range(tap_count):
        high, mid, low = split3(
            jnp.broadcast_to(columns[0:channels, t : t + 1], (channels, BLK))
        )
        weights.append(jnp.where(part < 2, high, jnp.where(part == 2, mid, low)))
    for d in range(planes):
        tile = jnp.zeros((channels, BLK), F32)
        for t in range(tap_count):
            tile = jnp.where(score == d - t + 1, weights[t], tile)
        band[d] = tile.astype(BF16)
    per_tile = BLK // channels
    for k in range(planes // per_tile):
        tile = band[k * per_tile : (k + 1) * per_tile].reshape(BLK, BLK)
        band_t[:, k * BLK : (k + 1) * BLK] = tile.astype(F32).T.astype(BF16)


def stage_kernel(features, views, features_out, views_out, sems):
    copies = [
        pltpu.make_async_copy(features, features_out, sems.at[0]),
        pltpu.make_async_copy(views, views_out, sems.at[1]),
    ]
    for copy in copies:
        copy.start()
    for copy in copies:
        copy.wait()


def side():
    return (lax.axis_index("frame") + lax.axis_index("tile")) % 2


def at_end():
    tile = lax.axis_index("tile")
    return jnp.where(side() == 0, tile == 0, tile == lax.axis_size("tile") - 1)


def halve_kernel(mine, partner, out):
    half = out.shape[1]

    def copy(start):
        for g, tile in enumerate((mine, partner)):
            for q in range(half):
                at = (start + q) * BLK
                out[g, q] = tile[0, :, at : at + BLK]

    pl.when(side() == 0)(lambda: copy(0))
    pl.when(side() == 1)(lambda: copy(half))


def rim_kernel(*refs):
    pieces, (outer, inner) = refs[:-2], refs[-2:]
    half = pieces[0].shape[1]
    left, right = slice(0, HB), slice(half - HB, half)

    def copy(out, part):
        for i, piece in enumerate(pieces):
            out[2 * i : 2 * i + 2] = piece[:, part]

    @pl.when(side() == 0)
    def _():
        copy(outer, left)
        copy(inner, right)

    @pl.when(side() == 1)
    def _():
        copy(outer, right)
        copy(inner, left)


def depth_kernel(views, offsets, offsets_partner, outer, inner, kernels, band, band_t, cot, cot_partner, *refs):
    (
        depth, depth_partner, core_grad, grad_outer, grad_inner,
        src, base, shifted, means, volume, ref_grad, sums, matrices, arrived,
    ) = refs[-14 - 2 * V : -2 * V]
    pieces, grads = refs[: -14 - 2 * V], refs[-2 * V :]
    slots, half = core_grad.shape[:2]
    channels, pixels = base.shape
    planes = kernels.shape[0]
    span = half + 2 * HB
    share = 1.0 / (V + 1)
    chunk = planes // CHUNKS
    me = lax.axis_index("frame")
    right_half = side()
    first_block = right_half * half
    where = (offsets, offsets_partner)
    columns = [(g, b) for g in range(2) for b in range(half)]

    def load(k):
        part = pl.ds(k * chunk, chunk)
        return pltpu.make_async_copy(kernels.at[part], matrices.at[part], arrived.at[k])

    for k in range(CHUNKS):
        load(k).start()

    def rims(near, far):
        for r in range(slots):
            src[r * span + near : r * span + near + HB] = outer[r]
            src[r * span + far : r * span + far + HB] = inner[r ^ 1]

    pl.when(right_half == 0)(lambda: rims(0, HB + half))
    pl.when(right_half == 1)(lambda: rims(HB + half, 0))

    @pl.when(at_end())
    def _():
        near = jnp.where(right_half == 0, 0, HB + half)
        for r in range(slots):
            for q in range(HB):
                src[r * span + q + near] = jnp.zeros((channels, BLK), BF16)

    for r in range(slots):
        src[r * span + HB : r * span + HB + half] = pieces[r // 2][r % 2]
    for k, (g, b) in enumerate(columns):
        base[:, k * BLK : (k + 1) * BLK] = pieces[0][g, b].astype(F32)
    for grad in grads:
        grad[...] = jnp.zeros_like(grad)
    ref_grad[...] = jnp.zeros_like(ref_grad)
    sums[...] = jnp.zeros_like(sums)
    slot_of = [[views[j, me ^ g] ^ me for j in range(V)] for g in range(2)]

    def rows_of(k, j):
        start = (k * V + j) * channels
        return slice(start, start + channels)

    def block_of(d, g, b, j):
        return where[g][0, j, first_block + b, d] + (b + HB)

    def forward(d):
        picked = []
        for g, b in columns:
            for j in range(V):
                picked.append(src[slot_of[g][j] * span + block_of(d, g, b, j)])
        warped = jnp.dot(
            jnp.concatenate(picked, axis=0), matrices[d], preferred_element_type=F32
        )
        for k in range(len(columns)):
            lanes = slice(k * BLK, (k + 1) * BLK)
            first = base[:, lanes]
            ys = [warped[rows_of(k, j)] - first for j in range(V)]
            for j in range(V):
                shifted[d, j, :, lanes] = ys[j]
            total = (ys[0] + ys[1]) + (ys[2] + ys[3])
            mean = total * share
            squares = (ys[0] * ys[0] + ys[1] * ys[1]) + (ys[2] * ys[2] + ys[3] * ys[3])
            variance = (squares - total * mean) * share
            volume[d, :, lanes] = variance.astype(BF16)
            means[d, :, lanes] = mean + (total - (V + 1) * mean) * share

    def forward_chunk(k, carry):
        load(k).wait()
        for i in range(chunk):
            forward(k * chunk + i)
        return carry

    lax.fori_loop(0, CHUNKS, forward_chunk, 0)

    wide = BLK * (2 if half % 2 == 0 else 1)
    groups = [slice(i, i + wide) for i in range(0, pixels, wide)]
    values = (
        lax.broadcasted_iota(jnp.int32, (planes, wide), 0).astype(F32) + 1.0
    ) / planes
    raws = []
    for lanes in groups:
        parts = jnp.dot(
            band_t[...], volume[:, :, lanes].reshape(planes * channels, wide),
            preferred_element_type=F32,
        )
        raws.append(
            parts[0:planes]
            + (parts[2 * planes : 3 * planes] + parts[3 * planes : 4 * planes])
        )
    stacks = []
    per_frame = half * BLK // wide
    for i, raw in enumerate(raws):
        given, out = ((cot, depth), (cot_partner, depth_partner))[i // per_frame]
        at = (i % per_frame) * wide
        slope_in = given[0:1, pl.ds(pl.multiple_of(first_block * BLK + at, BLK), wide)]
        tanh = jnp.tanh(raw)
        weights = jnp.exp(4.0 * tanh)
        norm = jnp.sum(weights, axis=0, keepdims=True)
        result = jnp.sum(weights * values, axis=0, keepdims=True) / norm
        out[0:1, at : at + wide] = result
        slope = (slope_in / norm) * (values - result) * weights
        draw = slope * (4.0 * (1.0 - tanh * tanh))
        high = draw.astype(BF16)
        low = (draw - high.astype(F32)).astype(BF16)
        stacks.append(jnp.concatenate([high, low, high, high], axis=0))
    for lanes, stack in zip(groups, stacks):
        dvolume = jnp.dot(
            band[...].reshape(planes * channels, BLK), stack, preferred_element_type=F32
        )
        volume[:, :, lanes] = dvolume.astype(BF16).reshape(planes, channels, wide)

    def backward(d, carry):
        rows = []
        for k in range(len(columns)):
            lanes = slice(k * BLK, (k + 1) * BLK)
            dvar = volume[d, :, lanes].astype(F32)
            mean = means[d, :, lanes]
            ref_grad[:, lanes] -= dvar * mean
            for j in range(V):
                rows.append((dvar * (shifted[d, j, :, lanes] - mean)).astype(BF16))
        dpicked = lax.dot_general(
            jnp.concatenate(rows, axis=0), matrices[d],
            (((1,), (1,)), ((), ())), preferred_element_type=F32,
        )
        for k, (g, b) in enumerate(columns):
            for j in range(V):
                grads[g * V + j][block_of(d, g, b, j)] += dpicked[rows_of(k, j)]
        return carry

    lax.fori_loop(0, planes, backward, 0, unroll=UNROLL)

    scale = 2.0 * share
    for k, (g, b) in enumerate(columns):
        sums[g, HB + b] = ref_grad[:, k * BLK : (k + 1) * BLK]
    for g in range(2):
        for j in range(V):
            sums[slot_of[g][j]] += grads[g * V + j][...]
    core_grad[...] = sums[:, HB : HB + half] * scale

    def give(left, right):
        left[...] = (sums[:, 0:HB] * scale).astype(BF16)
        right[...] = (sums[:, HB + half :] * scale).astype(BF16)

    pl.when(right_half == 0)(lambda: give(grad_outer, grad_inner))
    pl.when(right_half == 1)(lambda: give(grad_inner, grad_outer))


def merge_kernel(core, outer, inner, own, *sent):
    slots, half = core.shape[:2]

    def merge(near, far, beyond):
        for r in range(slots):
            out = own if r < 2 else sent[r // 2 - 1]
            for q in range(half):
                tile = core[r, q]
                if beyond and near <= q < near + HB:
                    tile = tile + outer[r, q - near].astype(F32)
                if far <= q < far + HB:
                    tile = tile + inner[r ^ 1, q - far].astype(F32)
                out[r % 2, q] = tile.astype(out.dtype)

    for i, ends in enumerate(((0, half - HB), (half - HB, 0))):
        here = side() == i
        pl.when(here & at_end())(lambda ends=ends: merge(*ends, False))
        pl.when(here & jnp.logical_not(at_end()))(lambda ends=ends: merge(*ends, True))


def sum_kernel(own, *refs):
    received, (mine, partner) = refs[:-2], refs[-2:]
    for g, out in enumerate((mine, partner)):
        total = own[g]
        for piece in received:
            total = total + piece[g].astype(F32)
        out[...] = total


def join_kernel(mine, partner, depth_mine, depth_partner, grad, depth):
    half = mine.shape[0]

    def join(at, tile, part):
        for q in range(half):
            grad[0, :, (at + q) * BLK : (at + q + 1) * BLK] = tile[q]
        depth[:, at * BLK : (at + half) * BLK] = part[...]

    @pl.when(side() == 0)
    def _():
        join(0, mine, depth_mine)
        join(half, partner, depth_partner)

    @pl.when(side() == 1)
    def _():
        join(0, partner, depth_partner)
        join(half, mine, depth_mine)


def exchange(x, distance):
    count = lax.axis_size("frame")
    return lax.ppermute(x, "frame", [(i, i ^ distance) for i in range(count)])


def swap_outer(x):
    count, tiles = lax.axis_size("frame"), lax.axis_size("tile")
    pairs = [
        (f * tiles + t, f * tiles + t + 1)
        for f in range(count)
        for t in range(tiles - 1)
        if (f + t) % 2 == 1
    ]
    ends = [(f, 0) for f in range(count) if f % 2 == 0]
    ends += [(f, tiles - 1) for f in range(count) if (f + tiles - 1) % 2 == 1]
    if count >= 4:
        pairs += [(f * tiles + t, (f ^ 2) * tiles + t) for f, t in ends if f & 2 == 0]
    return lax.ppermute(x, ("frame", "tile"), pairs + [(b, a) for a, b in pairs])


def small_call(kernel, ins, outs, scratch=()):
    return pl.pallas_call(
        kernel, out_shape=outs, in_specs=ins, out_specs=jax.tree.map(lambda _: VMEM, outs),
        scratch_shapes=scratch, compiler_params=SMALL,
    )


def per_device(features, views, offsets, kernels, reg_weight, head_weight, depth_cot):
    local_frames, channels, pixels = features.shape
    frames = lax.axis_size("frame")
    half = pixels // BLK // 2
    planes = kernels.shape[0]
    assert local_frames == 1 and frames & (frames - 1) == 0
    assert pixels == 2 * half * BLK and half >= HB
    shape = jax.ShapeDtypeStruct
    rim_shape = shape((frames, HB, channels, BLK), BF16)
    pair_shape = shape((2, half, channels, BLK), BF16)
    half_shape = shape((half, channels, BLK), F32)
    views = views.T
    offsets = jnp.swapaxes(offsets, 2, 3)

    band, band_t = small_call(
        weights_kernel, [SMEM, VMEM],
        (shape((planes, channels, BLK), BF16), shape((BLK, planes * channels), BF16)),
        [pltpu.VMEM((BLK, BLK), F32)],
    )(head_weight, reg_weight)

    features_partner = exchange(features, 1)
    staged, views = pl.pallas_call(
        stage_kernel,
        out_shape=(shape(features.shape, features.dtype), shape(views.shape, views.dtype)),
        in_specs=[pl.BlockSpec(memory_space=pltpu.HBM)] * 2,
        out_specs=(VMEM, VMEM),
        scratch_shapes=[pltpu.SemaphoreType.DMA((2,))],
        compiler_params=SMALL,
        name="stage_arguments",
    )(*(pltpu.with_memory_space_constraint(x, pltpu.HBM) for x in (features, views)))
    offsets_partner = exchange(offsets, 1)
    cot_partner = exchange(depth_cot, 1)
    pieces = [small_call(halve_kernel, [VMEM] * 2, pair_shape)(staged, features_partner)]
    for r in range(2, frames, 2):
        pieces.append(exchange(pieces[0], r))
    outer, inner = small_call(rim_kernel, [VMEM] * (frames // 2), (rim_shape, rim_shape))(*pieces)
    inner = exchange(inner, 1)
    outer = swap_outer(outer)

    span = half + 2 * HB
    depth_half = shape((1, half * BLK), F32)
    depth, depth_partner, core_grad, outer, inner = pl.pallas_call(
        depth_kernel,
        out_shape=(
            depth_half, depth_half, shape((frames, half, channels, BLK), F32), rim_shape, rim_shape,
        ),
        in_specs=[SMEM] * 3
        + [VMEM] * 2
        + [pl.BlockSpec(memory_space=pltpu.HBM)]
        + [VMEM] * (4 + frames // 2),
        out_specs=(VMEM,) * 5,
        scratch_shapes=[
            pltpu.VMEM((frames * span, channels, BLK), BF16),
            pltpu.VMEM((channels, pixels), F32),
            pltpu.VMEM((planes, V, channels, pixels), F32),
            pltpu.VMEM((planes, channels, pixels), F32),
            pltpu.VMEM((planes, channels, pixels), BF16),
            pltpu.VMEM((channels, pixels), F32),
            pltpu.VMEM((frames, span, channels, BLK), F32),
            pltpu.VMEM((planes, BLK, BLK), BF16),
            pltpu.SemaphoreType.DMA((CHUNKS,)),
        ]
        + [pltpu.VMEM((span, channels, BLK), F32)] * (2 * V),
        compiler_params=pltpu.CompilerParams(vmem_limit_bytes=34 << 20),
        cost_estimate=pl.CostEstimate(
            flops=4 * planes * V * channels * pixels * BLK, bytes_accessed=4 << 20,
            transcendentals=2 * planes * pixels,
        ),
        name="depth_window",
    )(
        views, offsets, offsets_partner, outer, inner,
        pltpu.with_memory_space_constraint(kernels, pltpu.HBM), band, band_t,
        depth_cot, cot_partner, *pieces,
    )

    inner = exchange(inner, 1)
    outer = swap_outer(outer)
    depth_partner = exchange(depth_partner, 1)
    own, *sent = small_call(
        merge_kernel, [VMEM] * 3,
        (shape(pair_shape.shape, F32),) + (pair_shape,) * (frames // 2 - 1),
    )(core_grad, outer, inner)
    received = []
    for r, piece in zip(range(2, frames, 2), sent):
        received.append(exchange(piece, r))
    mine, partner = small_call(
        sum_kernel, [VMEM] * (frames // 2), (half_shape, half_shape)
    )(own, *received)
    grad, depth = small_call(
        join_kernel, [VMEM] * 4,
        (shape(features.shape, F32), shape(depth_cot.shape, F32)),
    )(mine, exchange(partner, 1), depth, depth_partner)
    return depth, grad


def solution(mesh):
    return jax.shard_map(
        per_device,
        mesh=mesh,
        in_specs=(
            P("frame", None, "tile"),
            P(),
            P("frame", None, None, "tile"),
            P(),
            P(),
            P(),
            P("frame", "tile"),
        ),
        out_specs=(P("frame", "tile"), P("frame", None, "tile")),
        check_vma=False,
    )
```

```python
import jax
import jax.numpy as jnp
from jax import lax
from jax.experimental import pallas as pl
from jax.experimental.pallas import tpu as pltpu
from jax.sharding import PartitionSpec as P


V = 4
HB = 2
BLK = 128
FORWARD = 32
BACKWARD = 32
F32 = jnp.float32
BF16 = jnp.bfloat16
VMEM = pl.BlockSpec(memory_space=pltpu.VMEM)
SMEM = pl.BlockSpec(memory_space=pltpu.SMEM)
SMALL = pltpu.CompilerParams(vmem_limit_bytes=4 << 20)


def split3(w):
    high = w.astype(BF16).astype(F32)
    mid = (w - high).astype(BF16).astype(F32)
    return high, mid, w - high - mid


def weights_kernel(head, reg, kernels, band, band_t, matrices, rows, arrived):
    tap_count, hidden_count, channels = reg.shape
    planes = band.shape[0]
    load = pltpu.make_async_copy(kernels, matrices, arrived)
    load.start()
    rows[...] = jnp.zeros_like(rows)
    for t in range(tap_count):
        row = head[0] * reg[t, 0:1, :].astype(F32)
        for r in range(1, hidden_count):
            row = row + head[r] * reg[t, r : r + 1, :].astype(F32)
        rows[t : t + 1, 0:channels] = row
    columns = rows[...].T
    lane = lax.broadcasted_iota(jnp.int32, (channels, BLK), 1)
    part = lane // planes
    score = lane % planes
    weights = []
    for t in range(tap_count):
        high, mid, low = split3(
            jnp.broadcast_to(columns[0:channels, t : t + 1], (channels, BLK))
        )
        weights.append(jnp.where(part < 2, high, jnp.where(part == 2, mid, low)))
    for d in range(planes):
        tile = jnp.zeros((channels, BLK), F32)
        for t in range(tap_count):
            tile = jnp.where(score == d - t + 1, weights[t], tile)
        band[d] = tile.astype(BF16)
    per_tile = BLK // channels
    for k in range(planes // per_tile):
        tile = band[k * per_tile : (k + 1) * per_tile].reshape(BLK, BLK)
        band_t[:, k * BLK : (k + 1) * BLK] = tile.astype(F32).T.astype(BF16)
    load.wait()


def stage_kernel(*refs):
    count = len(refs) // 2
    sems = refs[-1]
    copies = [
        pltpu.make_async_copy(refs[i], refs[count + i], sems.at[i]) for i in range(count)
    ]
    for copy in copies:
        copy.start()
    for copy in copies:
        copy.wait()


def table_kernel(mine, partner, out):
    planes = mine.shape[3]
    half = mine.shape[2] // 2

    def fill(start):
        for g, offsets in enumerate((mine, partner)):
            for j in range(V):
                for b in range(half):
                    row = offsets[0, j, start + b : start + b + 1, :]
                    out[g * V + j : g * V + j + 1, b * planes : (b + 1) * planes] = row

    pl.when(side() == 0)(lambda: fill(0))
    pl.when(side() == 1)(lambda: fill(half))


def side():
    return (lax.axis_index("frame") + lax.axis_index("tile")) % 2


def at_end():
    tile = lax.axis_index("tile")
    return jnp.where(side() == 0, tile == 0, tile == lax.axis_size("tile") - 1)


def halve_kernel(mine, partner, out):
    half = out.shape[1]

    def copy(start):
        for g, tile in enumerate((mine, partner)):
            for q in range(half):
                at = (start + q) * BLK
                out[g, q] = tile[0, :, at : at + BLK]

    pl.when(side() == 0)(lambda: copy(0))
    pl.when(side() == 1)(lambda: copy(half))


def rim_kernel(*refs):
    pieces, (outer, inner) = refs[:-2], refs[-2:]
    half = pieces[0].shape[1]
    left, right = slice(0, HB), slice(half - HB, half)

    def copy(out, part):
        for i, piece in enumerate(pieces):
            out[2 * i : 2 * i + 2] = piece[:, part]

    @pl.when(side() == 0)
    def _():
        copy(outer, left)
        copy(inner, right)

    @pl.when(side() == 1)
    def _():
        copy(outer, right)
        copy(inner, left)


class Work:
    def __init__(self, views, table, matrices, half, far):
        self.table, self.matrices = table, matrices
        self.half, self.slots = half, lax.axis_size("frame")
        self.planes = matrices.shape[0]
        self.span = half + 2 * HB
        self.me, self.side = lax.axis_index("frame"), side()
        blocks = half - HB if far else HB
        self.first = jnp.where((self.side == 0) == far, HB if far else half - HB, 0)
        self.columns = [(g, b) for g in range(2) for b in range(blocks)]
        self.slot_of = [[views[j, self.me ^ g] ^ self.me for j in range(V)] for g in range(2)]

    def lanes(self, k):
        return slice(k * BLK, (k + 1) * BLK)

    def rows_of(self, k, i, channels):
        start = (k * (V // 2) + i) * channels
        return slice(start, start + channels)

    def block_of(self, d, g, b, j):
        at = self.first + b
        return self.table[g * V + j, at * self.planes + d] + (at + HB)

    def pair_matrix(self, d):
        matrix = self.matrices[d]
        upper = jnp.concatenate([matrix, matrix], axis=1)
        return jnp.concatenate([upper, jnp.concatenate([matrix, -matrix], axis=1)], axis=0)

    def gather(self, src, base, pieces, outer, inner):
        half, span = self.half, self.span
        for r in range(self.slots):
            src[r * span + HB : r * span + HB + half] = pieces[r // 2][r % 2]

        def rims(near, far):
            for r in range(self.slots):
                if outer is not None:
                    src[r * span + near : r * span + near + HB] = outer[r]
                src[r * span + far : r * span + far + HB] = inner[r ^ 1]

        pl.when(self.side == 0)(lambda: rims(0, HB + half))
        pl.when(self.side == 1)(lambda: rims(HB + half, 0))
        if outer is not None:

            @pl.when(at_end())
            def _():
                near = jnp.where(self.side == 0, 0, HB + half)
                for r in range(self.slots):
                    for q in range(HB):
                        src[r * span + q + near] = jnp.zeros_like(src[0])

        for k, (g, b) in enumerate(self.columns):
            base[:, self.lanes(k)] = 2.0 * pieces[0][g, self.first + b].astype(F32)

    def forward(self, src, base, shifted, means, volume):
        pairs, share = V // 2, 1.0 / (V + 1)
        channels = base.shape[0]

        def plane(d, carry):
            picked = []
            for g, b in self.columns:
                for i in range(pairs):
                    tiles = [
                        src[self.slot_of[g][j] * self.span + self.block_of(d, g, b, j)]
                        for j in (2 * i, 2 * i + 1)
                    ]
                    picked.append(jnp.concatenate(tiles, axis=1))
            warped = jnp.dot(
                jnp.concatenate(picked, axis=0), self.pair_matrix(d), preferred_element_type=F32
            )
            for k in range(len(self.columns)):
                lanes = self.lanes(k)
                rows = [self.rows_of(k, i, channels) for i in range(pairs)]
                twice_first = base[:, lanes]
                plus = [warped[rows[i], 0:BLK] - twice_first for i in range(pairs)]
                minus = [warped[rows[i], BLK:] for i in range(pairs)]
                for i in range(pairs):
                    shifted[d, 2 * i, :, lanes] = plus[i]
                    shifted[d, 2 * i + 1, :, lanes] = minus[i]
                total = sum(plus[1:], plus[0])
                twice_mean = total * (2.0 * share)
                squares = sum(x * x for x in plus) + sum(x * x for x in minus)
                variance = (squares - total * twice_mean) * (0.5 * share)
                volume[d, :, lanes] = variance.astype(BF16)
                centred = total - (0.5 / share) * twice_mean
                means[d, :, lanes] = twice_mean + centred * (2.0 * share)
            return carry

        lax.fori_loop(0, self.planes, plane, 0, unroll=FORWARD)

    def backward(self, shifted, means, dvolume, ref_grad, grads, sums):
        pairs = V // 2
        channels = ref_grad.shape[0]
        for grad in grads:
            grad[...] = jnp.zeros_like(grad)
        ref_grad[...] = jnp.zeros_like(ref_grad)

        def plane(d, carry):
            rows = []
            for k in range(len(self.columns)):
                lanes = self.lanes(k)
                dvar = dvolume[d, :, lanes].astype(F32)
                twice_mean = means[d, :, lanes]
                ref_grad[:, lanes] -= dvar * twice_mean
                for i in range(pairs):
                    plus = dvar * (shifted[d, 2 * i, :, lanes] - twice_mean)
                    minus = dvar * shifted[d, 2 * i + 1, :, lanes]
                    rows.append(
                        jnp.concatenate([plus.astype(BF16), minus.astype(BF16)], axis=1)
                    )
            dpicked = lax.dot_general(
                jnp.concatenate(rows, axis=0), self.pair_matrix(d),
                (((1,), (1,)), ((), ())), preferred_element_type=F32,
            )
            for k, (g, b) in enumerate(self.columns):
                for i in range(pairs):
                    for j, part in ((2 * i, slice(0, BLK)), (2 * i + 1, slice(BLK, None))):
                        grads[g * V + j][self.block_of(d, g, b, j)] += dpicked[
                            self.rows_of(k, i, channels), part
                        ]
            return carry

        lax.fori_loop(0, self.planes, plane, 0, unroll=BACKWARD)
        for k, (g, b) in enumerate(self.columns):
            sums[g * self.span + HB + self.first + b] += ref_grad[:, self.lanes(k)]
        for g in range(2):
            for j in range(V):
                sums[pl.ds(self.slot_of[g][j] * self.span, self.span)] += grads[g * V + j][...]

    def give(self, sums, out, outer):
        end = HB + self.half

        def copy(start):
            for r in range(self.slots):
                at = r * self.span + start
                out[r] = (sums[at : at + HB] * (1.0 / (V + 1))).astype(BF16)

        pl.when(self.side == 0)(lambda: copy(0 if outer else end))
        pl.when(self.side == 1)(lambda: copy(end if outer else 0))


def forward_kernel(views, table, inner, matrices, *refs):
    pieces, (shifted, means, volume, src, base) = refs[:-5], refs[-5:]
    work = Work(views, table, matrices, pieces[0].shape[1], True)
    work.gather(src, base, pieces, None, inner)
    work.forward(src, base, shifted, means, volume)


def depth_kernel(
    views, table, outer, inner, matrices, band, band_t, cot, cot_partner,
    far_volume, *refs,
):
    (
        depth, depth_partner, far_dvolume, grad_outer, sums,
        src, base, shifted, means, volume, ref_grad,
    ) = refs[-11 - 2 * V : -2 * V]
    pieces, grads = refs[: -11 - 2 * V], refs[-2 * V :]
    half = pieces[0].shape[1]
    planes = matrices.shape[0]
    channels = base.shape[0]
    near = Work(views, table, matrices, half, False)
    far = Work(views, table, matrices, half, True)
    near.gather(src, base, pieces, outer, inner)
    near.forward(src, base, shifted, means, volume)

    groups = []
    for work, given, taken in ((near, volume, volume), (far, far_volume, far_dvolume)):
        wide = len(work.columns) // 2 * BLK
        for g in range(2):
            groups.append((work, given, taken, slice(g * wide, (g + 1) * wide), wide, g))
    raws = []
    for work, given, _, lanes, wide, g in groups:
        parts = jnp.dot(
            band_t[...], given[:, :, lanes].reshape(planes * channels, wide),
            preferred_element_type=F32,
        )
        raws.append(
            parts[0:planes]
            + (parts[2 * planes : 3 * planes] + parts[3 * planes : 4 * planes])
        )
    stacks = []
    for (work, _, _, _, wide, g), raw in zip(groups, raws):
        values = (
            lax.broadcasted_iota(jnp.int32, (planes, wide), 0).astype(F32) + 1.0
        ) / planes
        start = pl.multiple_of(work.first * BLK, BLK)
        start_all = pl.multiple_of((work.side * half + work.first) * BLK, BLK)
        slope_in = (cot, cot_partner)[g][0:1, pl.ds(start_all, wide)]
        tanh = jnp.tanh(raw)
        weights = jnp.exp(4.0 * tanh)
        norm = jnp.sum(weights, axis=0, keepdims=True)
        result = jnp.sum(weights * values, axis=0, keepdims=True) / norm
        (depth, depth_partner)[g][0:1, pl.ds(start, wide)] = result
        slope = (slope_in / norm) * (values - result) * weights
        draw = slope * (4.0 * (1.0 - tanh * tanh))
        high = draw.astype(BF16)
        low = (draw - high.astype(F32)).astype(BF16)
        stacks.append(jnp.concatenate([high, low, high, high], axis=0))
    for (_, _, taken, lanes, wide, _), stack in zip(groups, stacks):
        dvolume = jnp.dot(
            band[...].reshape(planes * channels, BLK), stack, preferred_element_type=F32
        )
        taken[:, :, lanes] = dvolume.astype(BF16).reshape(planes, channels, wide)

    sums[...] = jnp.zeros_like(sums)
    near.backward(shifted, means, volume, ref_grad, grads, sums)
    near.give(sums, grad_outer, True)


def backward_kernel(
    views, table, matrices, shifted, means, dvolume, sums_in,
    core_grad, grad_inner, sums, ref_grad, *grads,
):
    half = core_grad.shape[1]
    work = Work(views, table, matrices, half, True)
    sums[...] = sums_in[...]
    work.backward(shifted, means, dvolume, ref_grad, grads, sums)
    for r in range(work.slots):
        at = r * work.span + HB
        core_grad[r] = sums[at : at + half] * (1.0 / (V + 1))
    work.give(sums, grad_inner, False)


def merge_kernel(core, outer, inner, own, *sent):
    slots, half = core.shape[:2]

    def merge(near, far, beyond):
        for r in range(slots):
            out = own if r < 2 else sent[r // 2 - 1]
            for q in range(half):
                tile = core[r, q]
                if beyond and near <= q < near + HB:
                    tile = tile + outer[r, q - near].astype(F32)
                if far <= q < far + HB:
                    tile = tile + inner[r ^ 1, q - far].astype(F32)
                out[r % 2, q] = tile.astype(out.dtype)

    for i, ends in enumerate(((0, half - HB), (half - HB, 0))):
        here = side() == i
        pl.when(here & at_end())(lambda ends=ends: merge(*ends, False))
        pl.when(here & jnp.logical_not(at_end()))(lambda ends=ends: merge(*ends, True))


def sum_kernel(own, *refs):
    received, (mine, partner) = refs[:-2], refs[-2:]
    for g, out in enumerate((mine, partner)):
        total = own[g]
        for piece in received:
            total = total + piece[g].astype(F32)
        out[...] = total.astype(out.dtype)


def join_kernel(mine, partner, depth_mine, depth_partner, grad, depth):
    half = mine.shape[0]

    def join(at, tile, part):
        for q in range(half):
            grad[0, :, (at + q) * BLK : (at + q + 1) * BLK] = tile[q].astype(F32)
        depth[:, at * BLK : (at + half) * BLK] = part[...]

    @pl.when(side() == 0)
    def _():
        join(0, mine, depth_mine)
        join(half, partner, depth_partner)

    @pl.when(side() == 1)
    def _():
        join(0, partner, depth_partner)
        join(half, mine, depth_mine)


def exchange(x, distance):
    count = lax.axis_size("frame")
    return lax.ppermute(x, "frame", [(i, i ^ distance) for i in range(count)])


def swap_outer(x):
    count, tiles = lax.axis_size("frame"), lax.axis_size("tile")
    pairs = [
        (f * tiles + t, f * tiles + t + 1)
        for f in range(count)
        for t in range(tiles - 1)
        if (f + t) % 2 == 1
    ]
    ends = [(f, 0) for f in range(count) if f % 2 == 0]
    ends += [(f, tiles - 1) for f in range(count) if (f + tiles - 1) % 2 == 1]
    if count >= 4:
        pairs += [(f * tiles + t, (f ^ 2) * tiles + t) for f, t in ends if f & 2 == 0]
    return lax.ppermute(x, ("frame", "tile"), pairs + [(b, a) for a, b in pairs])


def small_call(kernel, ins, outs, scratch=()):
    return pl.pallas_call(
        kernel, out_shape=outs, in_specs=ins, out_specs=jax.tree.map(lambda _: VMEM, outs),
        scratch_shapes=scratch, compiler_params=SMALL,
    )


def per_device(features, views, offsets, kernels, reg_weight, head_weight, depth_cot):
    local_frames, channels, pixels = features.shape
    frames = lax.axis_size("frame")
    half = pixels // BLK // 2
    planes = kernels.shape[0]
    assert local_frames == 1 and frames & (frames - 1) == 0
    assert pixels == 2 * half * BLK and half >= HB
    shape = jax.ShapeDtypeStruct
    rim_shape = shape((frames, HB, channels, BLK), BF16)
    pair_shape = shape((2, half, channels, BLK), BF16)
    half_shape = shape((half, channels, BLK), F32)
    views = views.T
    offsets = jnp.swapaxes(offsets, 2, 3)

    features_partner = exchange(features, 1)
    arguments = (features, views, reg_weight, head_weight, offsets, depth_cot)
    staged, views, reg_weight, head_weight, offsets_mine, cot_mine = pl.pallas_call(
        stage_kernel,
        out_shape=tuple(shape(x.shape, x.dtype) for x in arguments),
        in_specs=[pl.BlockSpec(memory_space=pltpu.HBM)] * len(arguments),
        out_specs=(VMEM,) * len(arguments),
        scratch_shapes=[pltpu.SemaphoreType.DMA((len(arguments),))],
        compiler_params=SMALL,
        name="stage_arguments",
    )(*(pltpu.with_memory_space_constraint(x, pltpu.HBM) for x in arguments))
    prepare = small_call(
        weights_kernel, [SMEM, VMEM, pl.BlockSpec(memory_space=pltpu.HBM)],
        (
            shape((planes, channels, BLK), BF16), shape((BLK, planes * channels), BF16),
            shape(kernels.shape, BF16),
        ),
        [pltpu.VMEM((BLK, BLK), F32), pltpu.SemaphoreType.DMA(())],
    )
    band, band_t, matrices = prepare(head_weight, reg_weight, pltpu.with_memory_space_constraint(kernels, pltpu.HBM))

    offsets_partner = exchange(offsets, 1)
    table = small_call(
        table_kernel, [VMEM] * 2, shape((2 * V, half * planes), jnp.int32)
    )(offsets_mine, offsets_partner)
    cot_partner = exchange(depth_cot, 1)
    pieces = [small_call(halve_kernel, [VMEM] * 2, pair_shape)(staged, features_partner)]
    for r in range(2, frames, 2):
        pieces.append(exchange(pieces[0], r))
    outer, inner = small_call(rim_kernel, [VMEM] * (frames // 2), (rim_shape, rim_shape))(*pieces)
    inner = exchange(inner, 1)
    outer = swap_outer(outer)

    span = half + 2 * HB
    assert V % 2 == 0 and planes % FORWARD == 0
    near_pixels, far_pixels = 2 * HB * BLK, 2 * (half - HB) * BLK
    depth_half = shape((1, half * BLK), F32)
    sums_shape = shape((frames * span, channels, BLK), F32)
    sources = pltpu.VMEM((frames * span, channels, BLK), BF16)
    accumulators = [pltpu.VMEM((span, channels, BLK), F32)] * (2 * V)

    def big_call(kernel, smem, vmem, outs, scratch, limit, part):
        return pl.pallas_call(
            kernel, out_shape=outs, in_specs=[SMEM] * smem + [VMEM] * vmem,
            out_specs=jax.tree.map(lambda _: VMEM, outs), scratch_shapes=scratch,
            compiler_params=pltpu.CompilerParams(vmem_limit_bytes=limit << 20),
            cost_estimate=pl.CostEstimate(
                flops=int(part * planes * V * channels * pixels * BLK),
                bytes_accessed=4 << 20, transcendentals=2 * planes * pixels,
            ),
        )

    shifted, means, volume = big_call(
        forward_kernel, 2, 2 + frames // 2,
        (
            shape((planes, V, channels, far_pixels), F32),
            shape((planes, channels, far_pixels), F32),
            shape((planes, channels, far_pixels), BF16),
        ),
        [sources, pltpu.VMEM((channels, far_pixels), F32)], 4, 1,
    )(views, table, inner, matrices, *pieces)
    depth, depth_partner, dvolume, outer, sums = big_call(
        depth_kernel, 2, 8 + frames // 2,
        (
            depth_half, depth_half, shape((planes, channels, far_pixels), BF16), rim_shape,
            sums_shape,
        ),
        [
            sources,
            pltpu.VMEM((channels, near_pixels), F32),
            pltpu.VMEM((planes, V, channels, near_pixels), F32),
            pltpu.VMEM((planes, channels, near_pixels), F32),
            pltpu.VMEM((planes, channels, near_pixels), BF16),
            pltpu.VMEM((channels, near_pixels), F32),
        ]
        + accumulators, 20, 2,
    )(
        views, table, outer, inner, matrices, band, band_t, cot_mine,
        cot_partner, volume, *pieces,
    )
    outer = swap_outer(outer)
    core_grad, inner = big_call(
        backward_kernel, 2, 5,
        (shape((frames, half, channels, BLK), F32), rim_shape),
        [
            pltpu.VMEM(sums_shape.shape, F32), pltpu.VMEM((channels, far_pixels), F32),
        ]
        + accumulators, 6, 1,
    )(views, table, matrices, shifted, means, dvolume, sums)
    inner = exchange(inner, 1)
    depth_partner = exchange(depth_partner, 1)
    own, *sent = small_call(
        merge_kernel, [VMEM] * 3,
        (shape(pair_shape.shape, F32),) + (pair_shape,) * (frames // 2 - 1),
    )(core_grad, outer, inner)
    received = []
    for r, piece in zip(range(2, frames, 2), sent):
        received.append(exchange(piece, r))
    mine, partner = small_call(
        sum_kernel, [VMEM] * (frames // 2), (half_shape, shape(half_shape.shape, BF16))
    )(own, *received)
    grad, depth = small_call(
        join_kernel, [VMEM] * 4,
        (shape(features.shape, F32), shape(depth_cot.shape, F32)),
    )(mine, exchange(partner, 1), depth, depth_partner)
    return depth, grad


def solution(mesh):
    return jax.shard_map(
        per_device,
        mesh=mesh,
        in_specs=(
            P("frame", None, "tile"),
            P(),
            P("frame", None, None, "tile"),
            P(),
            P(),
            P(),
            P("frame", "tile"),
        ),
        out_specs=(P("frame", "tile"), P("frame", None, "tile")),
        check_vma=False,
    )
```

```python
import jax
import jax.numpy as jnp
from jax import lax
from jax.experimental import pallas as pl
from jax.experimental.pallas import tpu as pltpu
from jax.sharding import PartitionSpec as P


V = 4
HB = 2
BLK = 128
FORWARD = 32
BACKWARD = 32
F32 = jnp.float32
BF16 = jnp.bfloat16
VMEM = pl.BlockSpec(memory_space=pltpu.VMEM)
SMEM = pl.BlockSpec(memory_space=pltpu.SMEM)
SMALL = pltpu.CompilerParams(vmem_limit_bytes=4 << 20)


def split3(w):
    high = w.astype(BF16).astype(F32)
    mid = (w - high).astype(BF16).astype(F32)
    return high, mid, w - high - mid


def weights_kernel(head, reg, kernels, band, band_t, matrices, rows, arrived):
    tap_count, hidden_count, channels = reg.shape
    planes = band.shape[0]
    load = pltpu.make_async_copy(kernels, matrices, arrived)
    load.start()
    rows[...] = jnp.zeros_like(rows)
    for t in range(tap_count):
        row = head[0] * reg[t, 0:1, :].astype(F32)
        for r in range(1, hidden_count):
            row = row + head[r] * reg[t, r : r + 1, :].astype(F32)
        rows[t : t + 1, 0:channels] = row
    columns = rows[...].T
    lane = lax.broadcasted_iota(jnp.int32, (channels, BLK), 1)
    part = lane // planes
    score = lane % planes
    weights = []
    for t in range(tap_count):
        high, mid, low = split3(
            jnp.broadcast_to(columns[0:channels, t : t + 1], (channels, BLK))
        )
        weights.append(jnp.where(part < 2, high, jnp.where(part == 2, mid, low)))
    for d in range(planes):
        tile = jnp.zeros((channels, BLK), F32)
        for t in range(tap_count):
            tile = jnp.where(score == d - t + 1, weights[t], tile)
        band[d] = tile.astype(BF16)
    per_tile = BLK // channels
    for k in range(planes // per_tile):
        tile = band[k * per_tile : (k + 1) * per_tile].reshape(BLK, BLK)
        band_t[:, k * BLK : (k + 1) * BLK] = tile.astype(F32).T.astype(BF16)
    load.wait()


def stage_kernel(*refs):
    count = len(refs) // 2
    sems = refs[-1]
    copies = [
        pltpu.make_async_copy(refs[i], refs[count + i], sems.at[i]) for i in range(count)
    ]
    for copy in copies:
        copy.start()
    for copy in copies:
        copy.wait()


def table_kernel(mine, partner, out):
    planes = mine.shape[3]
    half = mine.shape[2] // 2

    def fill(start):
        for g, offsets in enumerate((mine, partner)):
            for j in range(V):
                for b in range(half):
                    row = offsets[0, j, start + b : start + b + 1, :]
                    out[g * V + j : g * V + j + 1, b * planes : (b + 1) * planes] = row

    pl.when(side() == 0)(lambda: fill(0))
    pl.when(side() == 1)(lambda: fill(half))


def side():
    return (lax.axis_index("frame") + lax.axis_index("tile")) % 2


def at_end():
    tile = lax.axis_index("tile")
    return jnp.where(side() == 0, tile == 0, tile == lax.axis_size("tile") - 1)


def halve_kernel(mine, partner, out):
    half = out.shape[1]

    def copy(start):
        for g, tile in enumerate((mine, partner)):
            for q in range(half):
                at = (start + q) * BLK
                out[g, q] = tile[0, :, at : at + BLK]

    pl.when(side() == 0)(lambda: copy(0))
    pl.when(side() == 1)(lambda: copy(half))


def rim_kernel(*refs):
    pieces, (outer, inner) = refs[:-2], refs[-2:]
    half = pieces[0].shape[1]
    left, right = slice(0, HB), slice(half - HB, half)

    def copy(out, part):
        for i, piece in enumerate(pieces):
            out[2 * i : 2 * i + 2] = piece[:, part]

    @pl.when(side() == 0)
    def _():
        copy(outer, left)
        copy(inner, right)

    @pl.when(side() == 1)
    def _():
        copy(outer, right)
        copy(inner, left)


class Work:
    def __init__(self, views, table, matrices, half, far):
        self.table, self.matrices = table, matrices
        self.half, self.slots = half, lax.axis_size("frame")
        self.planes = matrices.shape[0]
        self.span = half + 2 * HB
        self.me, self.side = lax.axis_index("frame"), side()
        blocks = half - HB if far else HB
        self.first = jnp.where((self.side == 0) == far, HB if far else half - HB, 0)
        self.columns = [(g, b) for g in range(2) for b in range(blocks)]
        self.slot_of = [[views[j, self.me ^ g] ^ self.me for j in range(V)] for g in range(2)]

    def lanes(self, k):
        return slice(k * BLK, (k + 1) * BLK)

    def rows_of(self, k, i, channels):
        start = (k * (V // 2) + i) * channels
        return slice(start, start + channels)

    def block_of(self, d, g, b, j):
        at = self.first + b
        return self.table[g * V + j, at * self.planes + d] + (at + HB)

    def pair_matrix(self, d):
        matrix = self.matrices[d]
        upper = jnp.concatenate([matrix, matrix], axis=1)
        return jnp.concatenate([upper, jnp.concatenate([matrix, -matrix], axis=1)], axis=0)

    def gather(self, src, base, pieces, outer, inner):
        half, span = self.half, self.span
        for r in range(self.slots):
            src[r * span + HB : r * span + HB + half] = pieces[r // 2][r % 2]

        def rims(near, far):
            for r in range(self.slots):
                if outer is not None:
                    src[r * span + near : r * span + near + HB] = outer[r]
                src[r * span + far : r * span + far + HB] = inner[r ^ 1]

        pl.when(self.side == 0)(lambda: rims(0, HB + half))
        pl.when(self.side == 1)(lambda: rims(HB + half, 0))
        if outer is not None:

            @pl.when(at_end())
            def _():
                near = jnp.where(self.side == 0, 0, HB + half)
                for r in range(self.slots):
                    for q in range(HB):
                        src[r * span + q + near] = jnp.zeros_like(src[0])

        for k, (g, b) in enumerate(self.columns):
            base[:, self.lanes(k)] = 2.0 * pieces[0][g, self.first + b].astype(F32)

    def forward(self, src, base, shifted, means, volume):
        pairs, share = V // 2, 1.0 / (V + 1)
        channels = base.shape[0]

        def plane(d, carry):
            picked = []
            for g, b in self.columns:
                for i in range(pairs):
                    tiles = [
                        src[self.slot_of[g][j] * self.span + self.block_of(d, g, b, j)]
                        for j in (2 * i, 2 * i + 1)
                    ]
                    picked.append(jnp.concatenate(tiles, axis=1))
            warped = jnp.dot(
                jnp.concatenate(picked, axis=0), self.pair_matrix(d), preferred_element_type=F32
            )
            for k in range(len(self.columns)):
                lanes = self.lanes(k)
                rows = [self.rows_of(k, i, channels) for i in range(pairs)]
                twice_first = base[:, lanes]
                plus = [warped[rows[i], 0:BLK] - twice_first for i in range(pairs)]
                minus = [warped[rows[i], BLK:] for i in range(pairs)]
                for i in range(pairs):
                    shifted[d, 2 * i, :, lanes] = plus[i]
                    shifted[d, 2 * i + 1, :, lanes] = minus[i]
                total = sum(plus[1:], plus[0])
                twice_mean = total * (2.0 * share)
                squares = sum(x * x for x in plus) + sum(x * x for x in minus)
                variance = (squares - total * twice_mean) * (0.5 * share)
                volume[d, :, lanes] = variance.astype(BF16)
                centred = total - (0.5 / share) * twice_mean
                means[d, :, lanes] = twice_mean + centred * (2.0 * share)
            return carry

        lax.fori_loop(0, self.planes, plane, 0, unroll=FORWARD)

    def depths(self, band, band_t, cots, volume, dvolume, depths, first):
        planes = self.planes
        channels = volume.shape[1]
        wide = len(self.columns) // 2 * BLK
        groups = [slice(g * wide, (g + 1) * wide) for g in range(2)]
        values = (
            lax.broadcasted_iota(jnp.int32, (planes, wide), 0).astype(F32) + 1.0
        ) / planes
        raws = []
        for lanes in groups:
            parts = jnp.dot(
                band_t[...], volume[:, :, lanes].reshape(planes * channels, wide),
                preferred_element_type=F32,
            )
            raws.append(
                parts[0:planes]
                + (parts[2 * planes : 3 * planes] + parts[3 * planes : 4 * planes])
            )
        stacks = []
        start = first * BLK
        start_cot = pl.multiple_of((self.side * self.half + self.first) * BLK, BLK)
        for g, raw in enumerate(raws):
            slope_in = cots[g][0:1, pl.ds(start_cot, wide)]
            tanh = jnp.tanh(raw)
            weights = jnp.exp(4.0 * tanh)
            norm = jnp.sum(weights, axis=0, keepdims=True)
            result = jnp.sum(weights * values, axis=0, keepdims=True) / norm
            depths[g][0:1, pl.ds(pl.multiple_of(start, BLK), wide)] = result
            slope = (slope_in / norm) * (values - result) * weights
            draw = slope * (4.0 * (1.0 - tanh * tanh))
            high = draw.astype(BF16)
            low = (draw - high.astype(F32)).astype(BF16)
            stacks.append(jnp.concatenate([high, low, high, high], axis=0))
        for lanes, stack in zip(groups, stacks):
            cotangent = jnp.dot(
                band[...].reshape(planes * channels, BLK), stack, preferred_element_type=F32
            )
            dvolume[:, :, lanes] = cotangent.astype(BF16).reshape(planes, channels, wide)

    def backward(self, shifted, means, dvolume, ref_grad, grads, sums):
        pairs = V // 2
        channels = ref_grad.shape[0]
        for grad in grads:
            grad[...] = jnp.zeros_like(grad)
        ref_grad[...] = jnp.zeros_like(ref_grad)

        def plane(d, carry):
            rows = []
            for k in range(len(self.columns)):
                lanes = self.lanes(k)
                dvar = dvolume[d, :, lanes].astype(F32)
                twice_mean = means[d, :, lanes]
                ref_grad[:, lanes] -= dvar * twice_mean
                for i in range(pairs):
                    plus = dvar * (shifted[d, 2 * i, :, lanes] - twice_mean)
                    minus = dvar * shifted[d, 2 * i + 1, :, lanes]
                    rows.append(
                        jnp.concatenate([plus.astype(BF16), minus.astype(BF16)], axis=1)
                    )
            dpicked = lax.dot_general(
                jnp.concatenate(rows, axis=0), self.pair_matrix(d),
                (((1,), (1,)), ((), ())), preferred_element_type=F32,
            )
            for k, (g, b) in enumerate(self.columns):
                for i in range(pairs):
                    for j, part in ((2 * i, slice(0, BLK)), (2 * i + 1, slice(BLK, None))):
                        grads[g * V + j][self.block_of(d, g, b, j)] += dpicked[
                            self.rows_of(k, i, channels), part
                        ]
            return carry

        lax.fori_loop(0, self.planes, plane, 0, unroll=BACKWARD)
        for k, (g, b) in enumerate(self.columns):
            sums[g * self.span + HB + self.first + b] += ref_grad[:, self.lanes(k)]
        for g in range(2):
            for j in range(V):
                sums[pl.ds(self.slot_of[g][j] * self.span, self.span)] += grads[g * V + j][...]

    def give(self, sums, out, outer):
        end = HB + self.half

        def copy(start):
            for r in range(self.slots):
                at = r * self.span + start
                out[r] = (sums[at : at + HB] * (1.0 / (V + 1))).astype(BF16)

        pl.when(self.side == 0)(lambda: copy(0 if outer else end))
        pl.when(self.side == 1)(lambda: copy(end if outer else 0))


def forward_kernel(views, table, inner, matrices, band, band_t, cot, cot_partner, *refs):
    pieces, (shifted, means, dvolume, depth, depth_partner, src, base) = refs[:-7], refs[-7:]
    work = Work(views, table, matrices, pieces[0].shape[1], True)
    work.gather(src, base, pieces, None, inner)
    work.forward(src, base, shifted, means, dvolume)
    work.depths(
        band, band_t, (cot, cot_partner), dvolume, dvolume, (depth, depth_partner), 0
    )


def depth_kernel(
    views, table, outer, inner, matrices, band, band_t, cot, cot_partner, far_depth,
    far_depth_partner, *refs,
):
    (
        depth, depth_partner, grad_outer, sums,
        src, base, shifted, means, volume, ref_grad,
    ) = refs[-10 - 2 * V : -2 * V]
    pieces, grads = refs[: -10 - 2 * V], refs[-2 * V :]
    half = pieces[0].shape[1]
    near = Work(views, table, matrices, half, False)
    near.gather(src, base, pieces, outer, inner)
    near.forward(src, base, shifted, means, volume)
    near.depths(
        band, band_t, (cot, cot_partner), volume, volume, (depth, depth_partner), near.first
    )
    far_at = pl.multiple_of(jnp.where(near.side == 0, HB, 0) * BLK, BLK)
    far_wide = far_depth.shape[1]
    depth[0:1, pl.ds(far_at, far_wide)] = far_depth[...]
    depth_partner[0:1, pl.ds(far_at, far_wide)] = far_depth_partner[...]
    sums[...] = jnp.zeros_like(sums)
    near.backward(shifted, means, volume, ref_grad, grads, sums)
    near.give(sums, grad_outer, True)


def backward_kernel(
    views, table, matrices, shifted, means, dvolume, sums_in,
    core_grad, grad_inner, sums, ref_grad, *grads,
):
    half = core_grad.shape[1]
    work = Work(views, table, matrices, half, True)
    sums[...] = sums_in[...]
    work.backward(shifted, means, dvolume, ref_grad, grads, sums)
    for r in range(work.slots):
        at = r * work.span + HB
        core_grad[r] = sums[at : at + half] * (1.0 / (V + 1))
    work.give(sums, grad_inner, False)


def merge_kernel(core, outer, inner, own, *sent):
    slots, half = core.shape[:2]

    def merge(near, far, beyond):
        for r in range(slots):
            out = own if r < 2 else sent[r // 2 - 1]
            for q in range(half):
                tile = core[r, q]
                if beyond and near <= q < near + HB:
                    tile = tile + outer[r, q - near].astype(F32)
                if far <= q < far + HB:
                    tile = tile + inner[r ^ 1, q - far].astype(F32)
                out[r % 2, q] = tile.astype(out.dtype)

    for i, ends in enumerate(((0, half - HB), (half - HB, 0))):
        here = side() == i
        pl.when(here & at_end())(lambda ends=ends: merge(*ends, False))
        pl.when(here & jnp.logical_not(at_end()))(lambda ends=ends: merge(*ends, True))


def sum_kernel(own, *refs):
    received, (mine, partner) = refs[:-2], refs[-2:]
    for g, out in enumerate((mine, partner)):
        total = own[g]
        for piece in received:
            total = total + piece[g].astype(F32)
        out[...] = total.astype(out.dtype)


def join_kernel(mine, partner, depth_mine, depth_partner, grad, depth):
    half = mine.shape[0]

    def join(at, tile, part):
        for q in range(half):
            grad[0, :, (at + q) * BLK : (at + q + 1) * BLK] = tile[q].astype(F32)
        depth[:, at * BLK : (at + half) * BLK] = part[...]

    @pl.when(side() == 0)
    def _():
        join(0, mine, depth_mine)
        join(half, partner, depth_partner)

    @pl.when(side() == 1)
    def _():
        join(0, partner, depth_partner)
        join(half, mine, depth_mine)


def exchange(x, distance):
    count = lax.axis_size("frame")
    return lax.ppermute(x, "frame", [(i, i ^ distance) for i in range(count)])


def swap_outer(x):
    count, tiles = lax.axis_size("frame"), lax.axis_size("tile")
    pairs = [
        (f * tiles + t, f * tiles + t + 1)
        for f in range(count)
        for t in range(tiles - 1)
        if (f + t) % 2 == 1
    ]
    ends = [(f, 0) for f in range(count) if f % 2 == 0]
    ends += [(f, tiles - 1) for f in range(count) if (f + tiles - 1) % 2 == 1]
    if count >= 4:
        pairs += [(f * tiles + t, (f ^ 2) * tiles + t) for f, t in ends if f & 2 == 0]
    return lax.ppermute(x, ("frame", "tile"), pairs + [(b, a) for a, b in pairs])


def small_call(kernel, ins, outs, scratch=()):
    return pl.pallas_call(
        kernel, out_shape=outs, in_specs=ins, out_specs=jax.tree.map(lambda _: VMEM, outs),
        scratch_shapes=scratch, compiler_params=SMALL,
    )


def per_device(features, views, offsets, kernels, reg_weight, head_weight, depth_cot):
    local_frames, channels, pixels = features.shape
    frames = lax.axis_size("frame")
    half = pixels // BLK // 2
    planes = kernels.shape[0]
    assert local_frames == 1 and frames & (frames - 1) == 0
    assert pixels == 2 * half * BLK and half >= HB
    shape = jax.ShapeDtypeStruct
    rim_shape = shape((frames, HB, channels, BLK), BF16)
    pair_shape = shape((2, half, channels, BLK), BF16)
    half_shape = shape((half, channels, BLK), F32)
    views = views.T
    offsets = jnp.swapaxes(offsets, 2, 3)

    features_partner = exchange(features, 1)
    arguments = (features, views, reg_weight, head_weight, offsets, depth_cot)
    staged, views, reg_weight, head_weight, offsets_mine, cot_mine = pl.pallas_call(
        stage_kernel,
        out_shape=tuple(shape(x.shape, x.dtype) for x in arguments),
        in_specs=[pl.BlockSpec(memory_space=pltpu.HBM)] * len(arguments),
        out_specs=(VMEM,) * len(arguments),
        scratch_shapes=[pltpu.SemaphoreType.DMA((len(arguments),))],
        compiler_params=SMALL,
        name="stage_arguments",
    )(*(pltpu.with_memory_space_constraint(x, pltpu.HBM) for x in arguments))
    prepare = small_call(
        weights_kernel, [SMEM, VMEM, pl.BlockSpec(memory_space=pltpu.HBM)],
        (
            shape((planes, channels, BLK), BF16), shape((BLK, planes * channels), BF16),
            shape(kernels.shape, BF16),
        ),
        [pltpu.VMEM((BLK, BLK), F32), pltpu.SemaphoreType.DMA(())],
    )
    band, band_t, matrices = prepare(head_weight, reg_weight, pltpu.with_memory_space_constraint(kernels, pltpu.HBM))

    offsets_partner = exchange(offsets, 1)
    table = small_call(
        table_kernel, [VMEM] * 2, shape((2 * V, half * planes), jnp.int32)
    )(offsets_mine, offsets_partner)
    cot_partner = exchange(depth_cot, 1)
    pieces = [small_call(halve_kernel, [VMEM] * 2, pair_shape)(staged, features_partner)]
    for r in range(2, frames, 2):
        pieces.append(exchange(pieces[0], r))
    outer, inner = small_call(rim_kernel, [VMEM] * (frames // 2), (rim_shape, rim_shape))(*pieces)
    inner = exchange(inner, 1)
    outer = swap_outer(outer)

    span = half + 2 * HB
    assert V % 2 == 0 and planes % FORWARD == 0
    near_pixels, far_pixels = 2 * HB * BLK, 2 * (half - HB) * BLK
    depth_half = shape((1, half * BLK), F32)
    sums_shape = shape((frames * span, channels, BLK), F32)
    sources = pltpu.VMEM((frames * span, channels, BLK), BF16)
    accumulators = [pltpu.VMEM((span, channels, BLK), F32)] * (2 * V)

    def big_call(kernel, smem, vmem, outs, scratch, limit, part):
        return pl.pallas_call(
            kernel, out_shape=outs, in_specs=[SMEM] * smem + [VMEM] * vmem,
            out_specs=jax.tree.map(lambda _: VMEM, outs), scratch_shapes=scratch,
            compiler_params=pltpu.CompilerParams(vmem_limit_bytes=limit << 20),
            cost_estimate=pl.CostEstimate(
                flops=int(part * planes * V * channels * pixels * BLK),
                bytes_accessed=4 << 20, transcendentals=2 * planes * pixels,
            ),
        )

    far_half = shape((1, far_pixels // 2), F32)
    shifted, means, dvolume, *far_depths = big_call(
        forward_kernel, 2, 6 + frames // 2,
        (
            shape((planes, V, channels, far_pixels), F32),
            shape((planes, channels, far_pixels), F32),
            shape((planes, channels, far_pixels), BF16),
            far_half, far_half,
        ),
        [sources, pltpu.VMEM((channels, far_pixels), F32)], 4, 1,
    )(views, table, inner, matrices, band, band_t, cot_mine, cot_partner, *pieces)
    depth, depth_partner, outer, sums = big_call(
        depth_kernel, 2, 9 + frames // 2,
        (depth_half, depth_half, rim_shape, sums_shape),
        [
            sources,
            pltpu.VMEM((channels, near_pixels), F32),
            pltpu.VMEM((planes, V, channels, near_pixels), F32),
            pltpu.VMEM((planes, channels, near_pixels), F32),
            pltpu.VMEM((planes, channels, near_pixels), BF16),
            pltpu.VMEM((channels, near_pixels), F32),
        ]
        + accumulators, 20, 2,
    )(
        views, table, outer, inner, matrices, band, band_t, cot_mine, cot_partner,
        *far_depths, *pieces,
    )
    outer = swap_outer(outer)
    core_grad, inner = big_call(
        backward_kernel, 2, 5,
        (shape((frames, half, channels, BLK), F32), rim_shape),
        [
            pltpu.VMEM(sums_shape.shape, F32), pltpu.VMEM((channels, far_pixels), F32),
        ]
        + accumulators, 6, 1,
    )(views, table, matrices, shifted, means, dvolume, sums)
    inner = exchange(inner, 1)
    depth_partner = exchange(depth_partner, 1)
    own, *sent = small_call(
        merge_kernel, [VMEM] * 3,
        (shape(pair_shape.shape, F32),) + (pair_shape,) * (frames // 2 - 1),
    )(core_grad, outer, inner)
    received = []
    for r, piece in zip(range(2, frames, 2), sent):
        received.append(exchange(piece, r))
    mine, partner = small_call(
        sum_kernel, [VMEM] * (frames // 2), (half_shape, shape(half_shape.shape, BF16))
    )(own, *received)
    grad, depth = small_call(
        join_kernel, [VMEM] * 4,
        (shape(features.shape, F32), shape(depth_cot.shape, F32)),
    )(mine, exchange(partner, 1), depth, depth_partner)
    return depth, grad


def solution(mesh):
    return jax.shard_map(
        per_device,
        mesh=mesh,
        in_specs=(
            P("frame", None, "tile"),
            P(),
            P("frame", None, None, "tile"),
            P(),
            P(),
            P(),
            P("frame", "tile"),
        ),
        out_specs=(P("frame", "tile"), P("frame", None, "tile")),
        check_vma=False,
    )
```

```python
import jax
import jax.numpy as jnp
from jax import lax
from jax.experimental import pallas as pl
from jax.experimental.pallas import tpu as pltpu
from jax.sharding import PartitionSpec as P


V = 4
HB = 2
BLK = 128
FORWARD = 32
BACKWARD = 32
F32 = jnp.float32
BF16 = jnp.bfloat16
VMEM = pl.BlockSpec(memory_space=pltpu.VMEM)
SMEM = pl.BlockSpec(memory_space=pltpu.SMEM)
SMALL = pltpu.CompilerParams(vmem_limit_bytes=4 << 20)


def split3(w):
    high = w.astype(BF16).astype(F32)
    mid = (w - high).astype(BF16).astype(F32)
    return high, mid, w - high - mid


def weights_kernel(head, reg, kernels, band, band_t, matrices, rows, arrived):
    tap_count, hidden_count, channels = reg.shape
    planes = band.shape[0]
    load = pltpu.make_async_copy(kernels, matrices, arrived)
    load.start()
    rows[...] = jnp.zeros_like(rows)
    for t in range(tap_count):
        row = head[0] * reg[t, 0:1, :].astype(F32)
        for r in range(1, hidden_count):
            row = row + head[r] * reg[t, r : r + 1, :].astype(F32)
        rows[t : t + 1, 0:channels] = row
    columns = rows[...].T
    lane = lax.broadcasted_iota(jnp.int32, (channels, BLK), 1)
    part = lane // planes
    score = lane % planes
    weights = []
    for t in range(tap_count):
        high, mid, low = split3(
            jnp.broadcast_to(columns[0:channels, t : t + 1], (channels, BLK))
        )
        weights.append(jnp.where(part < 2, high, jnp.where(part == 2, mid, low)))
    for d in range(planes):
        tile = jnp.zeros((channels, BLK), F32)
        for t in range(tap_count):
            tile = jnp.where(score == d - t + 1, weights[t], tile)
        band[d] = tile.astype(BF16)
    per_tile = BLK // channels
    for k in range(planes // per_tile):
        tile = band[k * per_tile : (k + 1) * per_tile].reshape(BLK, BLK)
        band_t[:, k * BLK : (k + 1) * BLK] = tile.astype(F32).T.astype(BF16)
    load.wait()


def stage_kernel(*refs):
    count = len(refs) // 2
    sems = refs[-1]
    copies = [
        pltpu.make_async_copy(refs[i], refs[count + i], sems.at[i]) for i in range(count)
    ]
    for copy in copies:
        copy.start()
    for copy in copies:
        copy.wait()


def table_kernel(mine, partner, out):
    planes = mine.shape[3]
    half = mine.shape[2] // 2

    def fill(start):
        for g, offsets in enumerate((mine, partner)):
            for j in range(V):
                for b in range(half):
                    row = offsets[0, j, start + b : start + b + 1, :]
                    out[g * V + j : g * V + j + 1, b * planes : (b + 1) * planes] = row

    pl.when(side() == 0)(lambda: fill(0))
    pl.when(side() == 1)(lambda: fill(half))


def side():
    return (lax.axis_index("frame") + lax.axis_index("tile")) % 2


def at_end():
    tile = lax.axis_index("tile")
    return jnp.where(side() == 0, tile == 0, tile == lax.axis_size("tile") - 1)


def halve_kernel(mine, partner, out):
    half = out.shape[1]

    def copy(start):
        for g, tile in enumerate((mine, partner)):
            for q in range(half):
                at = (start + q) * BLK
                out[g, q] = tile[0, :, at : at + BLK]

    pl.when(side() == 0)(lambda: copy(0))
    pl.when(side() == 1)(lambda: copy(half))


def rim_kernel(*refs):
    pieces, (outer, inner) = refs[:-2], refs[-2:]
    half = pieces[0].shape[1]
    left, right = slice(0, HB), slice(half - HB, half)

    def copy(out, part):
        for i, piece in enumerate(pieces):
            out[2 * i : 2 * i + 2] = piece[:, part]

    @pl.when(side() == 0)
    def _():
        copy(outer, left)
        copy(inner, right)

    @pl.when(side() == 1)
    def _():
        copy(outer, right)
        copy(inner, left)


class Work:
    def __init__(self, views, table, matrices, half, far):
        self.table, self.matrices = table, matrices
        self.half, self.slots = half, lax.axis_size("frame")
        self.planes = matrices.shape[0]
        self.span = half + 2 * HB
        self.me, self.side = lax.axis_index("frame"), side()
        blocks = half - HB if far else HB
        self.first = jnp.where((self.side == 0) == far, HB if far else half - HB, 0)
        self.columns = [(g, b) for g in range(2) for b in range(blocks)]
        self.slot_of = [[views[j, self.me ^ g] ^ self.me for j in range(V)] for g in range(2)]

    def lanes(self, k):
        return slice(k * BLK, (k + 1) * BLK)

    def rows_of(self, k, i, channels):
        start = (k * (V // 2) + i) * channels
        return slice(start, start + channels)

    def block_of(self, d, g, b, j):
        at = self.first + b
        return self.table[g * V + j, at * self.planes + d] + (at + HB)

    def pair_matrix(self, d):
        matrix = self.matrices[d]
        upper = jnp.concatenate([matrix, matrix], axis=1)
        return jnp.concatenate([upper, jnp.concatenate([matrix, -matrix], axis=1)], axis=0)

    def gather(self, src, base, pieces, outer, inner):
        half, span = self.half, self.span
        for r in range(self.slots):
            src[r * span + HB : r * span + HB + half] = pieces[r // 2][r % 2]

        def rims(near, far):
            for r in range(self.slots):
                if outer is not None:
                    src[r * span + near : r * span + near + HB] = outer[r]
                src[r * span + far : r * span + far + HB] = inner[r ^ 1]

        pl.when(self.side == 0)(lambda: rims(0, HB + half))
        pl.when(self.side == 1)(lambda: rims(HB + half, 0))
        if outer is not None:

            @pl.when(at_end())
            def _():
                near = jnp.where(self.side == 0, 0, HB + half)
                for r in range(self.slots):
                    for q in range(HB):
                        src[r * span + q + near] = jnp.zeros_like(src[0])

        for k, (g, b) in enumerate(self.columns):
            base[:, self.lanes(k)] = 2.0 * pieces[0][g, self.first + b].astype(F32)

    def forward(self, src, base, shifted, means, volume):
        pairs, share = V // 2, 1.0 / (V + 1)
        channels = base.shape[0]

        def plane(d, carry):
            picked = []
            for g, b in self.columns:
                for i in range(pairs):
                    tiles = [
                        src[self.slot_of[g][j] * self.span + self.block_of(d, g, b, j)]
                        for j in (2 * i, 2 * i + 1)
                    ]
                    picked.append(jnp.concatenate(tiles, axis=1))
            warped = jnp.dot(
                jnp.concatenate(picked, axis=0), self.pair_matrix(d), preferred_element_type=F32
            )
            for k in range(len(self.columns)):
                lanes = self.lanes(k)
                rows = [self.rows_of(k, i, channels) for i in range(pairs)]
                twice_first = base[:, lanes]
                plus = [warped[rows[i], 0:BLK] - twice_first for i in range(pairs)]
                minus = [warped[rows[i], BLK:] for i in range(pairs)]
                for i in range(pairs):
                    shifted[d, 2 * i, :, lanes] = plus[i]
                    shifted[d, 2 * i + 1, :, lanes] = minus[i]
                total = sum(plus[1:], plus[0])
                twice_mean = total * (2.0 * share)
                squares = sum(x * x for x in plus) + sum(x * x for x in minus)
                variance = (squares - total * twice_mean) * (0.5 * share)
                volume[d, :, lanes] = variance.astype(BF16)
                centred = total - (0.5 / share) * twice_mean
                means[d, :, lanes] = twice_mean + centred * (2.0 * share)
            return carry

        lax.fori_loop(0, self.planes, plane, 0, unroll=FORWARD)

    def depths(self, band, band_t, cots, volume, dvolume, depths, first):
        planes = self.planes
        channels = volume.shape[1]
        wide = len(self.columns) // 2 * BLK
        groups = [slice(g * wide, (g + 1) * wide) for g in range(2)]
        values = (
            lax.broadcasted_iota(jnp.int32, (planes, wide), 0).astype(F32) + 1.0
        ) / planes
        raws = []
        for lanes in groups:
            parts = jnp.dot(
                band_t[...], volume[:, :, lanes].reshape(planes * channels, wide),
                preferred_element_type=F32,
            )
            raws.append(
                parts[0:planes]
                + (parts[2 * planes : 3 * planes] + parts[3 * planes : 4 * planes])
            )
        stacks = []
        start = first * BLK
        start_cot = pl.multiple_of((self.side * self.half + self.first) * BLK, BLK)
        for g, raw in enumerate(raws):
            slope_in = cots[g][0:1, pl.ds(start_cot, wide)]
            tanh = jnp.tanh(raw)
            weights = jnp.exp(4.0 * tanh)
            norm = jnp.sum(weights, axis=0, keepdims=True)
            result = jnp.sum(weights * values, axis=0, keepdims=True) / norm
            depths[g][0:1, pl.ds(pl.multiple_of(start, BLK), wide)] = result
            slope = (slope_in / norm) * (values - result) * weights
            draw = slope * (4.0 * (1.0 - tanh * tanh))
            high = draw.astype(BF16)
            low = (draw - high.astype(F32)).astype(BF16)
            stacks.append(jnp.concatenate([high, low, high, high], axis=0))
        for lanes, stack in zip(groups, stacks):
            cotangent = jnp.dot(
                band[...].reshape(planes * channels, BLK), stack, preferred_element_type=F32
            )
            dvolume[:, :, lanes] = cotangent.astype(BF16).reshape(planes, channels, wide)

    def backward(self, shifted, means, dvolume, ref_grad, grads, sums):
        pairs = V // 2
        channels = ref_grad.shape[0]
        for grad in grads:
            grad[...] = jnp.zeros_like(grad)
        ref_grad[...] = jnp.zeros_like(ref_grad)

        def plane(d, carry):
            rows = []
            for k in range(len(self.columns)):
                lanes = self.lanes(k)
                dvar = dvolume[d, :, lanes].astype(F32)
                twice_mean = means[d, :, lanes]
                ref_grad[:, lanes] -= dvar * twice_mean
                for i in range(pairs):
                    plus = dvar * (shifted[d, 2 * i, :, lanes] - twice_mean)
                    minus = dvar * shifted[d, 2 * i + 1, :, lanes]
                    rows += [(plus + minus).astype(BF16), (plus - minus).astype(BF16)]
            dpicked = lax.dot_general(
                jnp.concatenate(rows, axis=0), self.matrices[d],
                (((1,), (1,)), ((), ())), preferred_element_type=F32,
            )
            for k, (g, b) in enumerate(self.columns):
                for j in range(V):
                    start = (k * V + j) * channels
                    grads[g * V + j][self.block_of(d, g, b, j)] += dpicked[start : start + channels]
            return carry

        lax.fori_loop(0, self.planes, plane, 0, unroll=BACKWARD)
        for k, (g, b) in enumerate(self.columns):
            sums[g * self.span + HB + self.first + b] += ref_grad[:, self.lanes(k)]
        for g in range(2):
            for j in range(V):
                sums[pl.ds(self.slot_of[g][j] * self.span, self.span)] += grads[g * V + j][...]

    def give(self, sums, out, outer):
        end = HB + self.half

        def copy(start):
            for r in range(self.slots):
                at = r * self.span + start
                out[r] = (sums[at : at + HB] * (1.0 / (V + 1))).astype(BF16)

        pl.when(self.side == 0)(lambda: copy(0 if outer else end))
        pl.when(self.side == 1)(lambda: copy(end if outer else 0))


def forward_kernel(views, table, inner, matrices, band, band_t, cot, cot_partner, *refs):
    pieces, (shifted, means, dvolume, depth, depth_partner, src, base) = refs[:-7], refs[-7:]
    work = Work(views, table, matrices, pieces[0].shape[1], True)
    work.gather(src, base, pieces, None, inner)
    work.forward(src, base, shifted, means, dvolume)
    work.depths(
        band, band_t, (cot, cot_partner), dvolume, dvolume, (depth, depth_partner), 0
    )


def depth_kernel(
    views, table, outer, inner, matrices, band, band_t, cot, cot_partner, far_depth,
    far_depth_partner, *refs,
):
    (
        depth, depth_partner, grad_outer, sums,
        src, base, shifted, means, volume, ref_grad,
    ) = refs[-10 - 2 * V : -2 * V]
    pieces, grads = refs[: -10 - 2 * V], refs[-2 * V :]
    half = pieces[0].shape[1]
    near = Work(views, table, matrices, half, False)
    near.gather(src, base, pieces, outer, inner)
    near.forward(src, base, shifted, means, volume)
    near.depths(
        band, band_t, (cot, cot_partner), volume, volume, (depth, depth_partner), near.first
    )
    far_at = pl.multiple_of(jnp.where(near.side == 0, HB, 0) * BLK, BLK)
    far_wide = far_depth.shape[1]
    depth[0:1, pl.ds(far_at, far_wide)] = far_depth[...]
    depth_partner[0:1, pl.ds(far_at, far_wide)] = far_depth_partner[...]
    sums[...] = jnp.zeros_like(sums)
    near.backward(shifted, means, volume, ref_grad, grads, sums)
    near.give(sums, grad_outer, True)


def backward_kernel(
    views, table, matrices, shifted, means, dvolume, sums_in,
    core_grad, grad_inner, sums, ref_grad, *grads,
):
    half = core_grad.shape[1]
    work = Work(views, table, matrices, half, True)
    sums[...] = sums_in[...]
    work.backward(shifted, means, dvolume, ref_grad, grads, sums)
    for r in range(work.slots):
        at = r * work.span + HB
        core_grad[r] = sums[at : at + half] * (1.0 / (V + 1))
    work.give(sums, grad_inner, False)


def merge_kernel(core, outer, inner, own, *sent):
    slots, half = core.shape[:2]

    def merge(near, far, beyond):
        for r in range(slots):
            out = own if r < 2 else sent[r // 2 - 1]
            for q in range(half):
                tile = core[r, q]
                if beyond and near <= q < near + HB:
                    tile = tile + outer[r, q - near].astype(F32)
                if far <= q < far + HB:
                    tile = tile + inner[r ^ 1, q - far].astype(F32)
                out[r % 2, q] = tile.astype(out.dtype)

    for i, ends in enumerate(((0, half - HB), (half - HB, 0))):
        here = side() == i
        pl.when(here & at_end())(lambda ends=ends: merge(*ends, False))
        pl.when(here & jnp.logical_not(at_end()))(lambda ends=ends: merge(*ends, True))


def sum_kernel(own, *refs):
    received, (mine, partner) = refs[:-2], refs[-2:]
    for g, out in enumerate((mine, partner)):
        total = own[g]
        for piece in received:
            total = total + piece[g].astype(F32)
        out[...] = total.astype(out.dtype)


def join_kernel(mine, partner, depth_mine, depth_partner, grad, depth):
    half = mine.shape[0]

    def join(at, tile, part):
        for q in range(half):
            grad[0, :, (at + q) * BLK : (at + q + 1) * BLK] = tile[q].astype(F32)
        depth[:, at * BLK : (at + half) * BLK] = part[...]

    @pl.when(side() == 0)
    def _():
        join(0, mine, depth_mine)
        join(half, partner, depth_partner)

    @pl.when(side() == 1)
    def _():
        join(0, partner, depth_partner)
        join(half, mine, depth_mine)


def exchange(x, distance):
    count = lax.axis_size("frame")
    return lax.ppermute(x, "frame", [(i, i ^ distance) for i in range(count)])


def swap_outer(x):
    count, tiles = lax.axis_size("frame"), lax.axis_size("tile")
    pairs = [
        (f * tiles + t, f * tiles + t + 1)
        for f in range(count)
        for t in range(tiles - 1)
        if (f + t) % 2 == 1
    ]
    ends = [(f, 0) for f in range(count) if f % 2 == 0]
    ends += [(f, tiles - 1) for f in range(count) if (f + tiles - 1) % 2 == 1]
    if count >= 4:
        pairs += [(f * tiles + t, (f ^ 2) * tiles + t) for f, t in ends if f & 2 == 0]
    return lax.ppermute(x, ("frame", "tile"), pairs + [(b, a) for a, b in pairs])


def small_call(kernel, ins, outs, scratch=()):
    return pl.pallas_call(
        kernel, out_shape=outs, in_specs=ins, out_specs=jax.tree.map(lambda _: VMEM, outs),
        scratch_shapes=scratch, compiler_params=SMALL,
    )


def per_device(features, views, offsets, kernels, reg_weight, head_weight, depth_cot):
    local_frames, channels, pixels = features.shape
    frames = lax.axis_size("frame")
    half = pixels // BLK // 2
    planes = kernels.shape[0]
    assert local_frames == 1 and frames & (frames - 1) == 0
    assert pixels == 2 * half * BLK and half >= HB
    shape = jax.ShapeDtypeStruct
    rim_shape = shape((frames, HB, channels, BLK), BF16)
    pair_shape = shape((2, half, channels, BLK), BF16)
    half_shape = shape((half, channels, BLK), F32)
    views = views.T
    offsets = jnp.swapaxes(offsets, 2, 3)

    features_partner = exchange(features, 1)
    arguments = (features, views, reg_weight, head_weight, offsets, depth_cot)
    staged, views, reg_weight, head_weight, offsets_mine, cot_mine = pl.pallas_call(
        stage_kernel,
        out_shape=tuple(shape(x.shape, x.dtype) for x in arguments),
        in_specs=[pl.BlockSpec(memory_space=pltpu.HBM)] * len(arguments),
        out_specs=(VMEM,) * len(arguments),
        scratch_shapes=[pltpu.SemaphoreType.DMA((len(arguments),))],
        compiler_params=SMALL,
        name="stage_arguments",
    )(*(pltpu.with_memory_space_constraint(x, pltpu.HBM) for x in arguments))
    prepare = small_call(
        weights_kernel, [SMEM, VMEM, pl.BlockSpec(memory_space=pltpu.HBM)],
        (
            shape((planes, channels, BLK), BF16), shape((BLK, planes * channels), BF16),
            shape(kernels.shape, BF16),
        ),
        [pltpu.VMEM((BLK, BLK), F32), pltpu.SemaphoreType.DMA(())],
    )
    band, band_t, matrices = prepare(head_weight, reg_weight, pltpu.with_memory_space_constraint(kernels, pltpu.HBM))

    offsets_partner = exchange(offsets, 1)
    table = small_call(
        table_kernel, [VMEM] * 2, shape((2 * V, half * planes), jnp.int32)
    )(offsets_mine, offsets_partner)
    cot_partner = exchange(depth_cot, 1)
    pieces = [small_call(halve_kernel, [VMEM] * 2, pair_shape)(staged, features_partner)]
    for r in range(2, frames, 2):
        pieces.append(exchange(pieces[0], r))
    outer, inner = small_call(rim_kernel, [VMEM] * (frames // 2), (rim_shape, rim_shape))(*pieces)
    inner = exchange(inner, 1)
    outer = swap_outer(outer)

    span = half + 2 * HB
    assert V % 2 == 0 and planes % FORWARD == 0
    near_pixels, far_pixels = 2 * HB * BLK, 2 * (half - HB) * BLK
    depth_half = shape((1, half * BLK), F32)
    sums_shape = shape((frames * span, channels, BLK), F32)
    sources = pltpu.VMEM((frames * span, channels, BLK), BF16)
    accumulators = [pltpu.VMEM((span, channels, BLK), F32)] * (2 * V)

    def big_call(kernel, smem, vmem, outs, scratch, limit, part):
        return pl.pallas_call(
            kernel, out_shape=outs, in_specs=[SMEM] * smem + [VMEM] * vmem,
            out_specs=jax.tree.map(lambda _: VMEM, outs), scratch_shapes=scratch,
            compiler_params=pltpu.CompilerParams(vmem_limit_bytes=limit << 20),
            cost_estimate=pl.CostEstimate(
                flops=int(part * planes * V * channels * pixels * BLK),
                bytes_accessed=4 << 20, transcendentals=2 * planes * pixels,
            ),
        )

    far_half = shape((1, far_pixels // 2), F32)
    shifted, means, dvolume, *far_depths = big_call(
        forward_kernel, 2, 6 + frames // 2,
        (
            shape((planes, V, channels, far_pixels), F32),
            shape((planes, channels, far_pixels), F32),
            shape((planes, channels, far_pixels), BF16),
            far_half, far_half,
        ),
        [sources, pltpu.VMEM((channels, far_pixels), F32)], 4, 1,
    )(views, table, inner, matrices, band, band_t, cot_mine, cot_partner, *pieces)
    depth, depth_partner, outer, sums = big_call(
        depth_kernel, 2, 9 + frames // 2,
        (depth_half, depth_half, rim_shape, sums_shape),
        [
            sources,
            pltpu.VMEM((channels, near_pixels), F32),
            pltpu.VMEM((planes, V, channels, near_pixels), F32),
            pltpu.VMEM((planes, channels, near_pixels), F32),
            pltpu.VMEM((planes, channels, near_pixels), BF16),
            pltpu.VMEM((channels, near_pixels), F32),
        ]
        + accumulators, 20, 2,
    )(
        views, table, outer, inner, matrices, band, band_t, cot_mine, cot_partner,
        *far_depths, *pieces,
    )
    outer = swap_outer(outer)
    core_grad, inner = big_call(
        backward_kernel, 2, 5,
        (shape((frames, half, channels, BLK), F32), rim_shape),
        [
            pltpu.VMEM(sums_shape.shape, F32), pltpu.VMEM((channels, far_pixels), F32),
        ]
        + accumulators, 6, 1,
    )(views, table, matrices, shifted, means, dvolume, sums)
    inner = exchange(inner, 1)
    depth_partner = exchange(depth_partner, 1)
    own, *sent = small_call(
        merge_kernel, [VMEM] * 3,
        (shape(pair_shape.shape, F32),) + (pair_shape,) * (frames // 2 - 1),
    )(core_grad, outer, inner)
    received = []
    for r, piece in zip(range(2, frames, 2), sent):
        received.append(exchange(piece, r))
    mine, partner = small_call(
        sum_kernel, [VMEM] * (frames // 2), (half_shape, shape(half_shape.shape, BF16))
    )(own, *received)
    grad, depth = small_call(
        join_kernel, [VMEM] * 4,
        (shape(features.shape, F32), shape(depth_cot.shape, F32)),
    )(mine, exchange(partner, 1), depth, depth_partner)
    return depth, grad


def solution(mesh):
    return jax.shard_map(
        per_device,
        mesh=mesh,
        in_specs=(
            P("frame", None, "tile"),
            P(),
            P("frame", None, None, "tile"),
            P(),
            P(),
            P(),
            P("frame", "tile"),
        ),
        out_specs=(P("frame", "tile"), P("frame", None, "tile")),
        check_vma=False,
    )
```

```python
import jax
import jax.numpy as jnp
from jax import lax
from jax.experimental import pallas as pl
from jax.experimental.pallas import tpu as pltpu
from jax.sharding import PartitionSpec as P


V = 4
HB = 2
BLK = 128
FORWARD = 32
BACKWARD = 32
F32 = jnp.float32
BF16 = jnp.bfloat16
VMEM = pl.BlockSpec(memory_space=pltpu.VMEM)
SMEM = pl.BlockSpec(memory_space=pltpu.SMEM)
SMALL = pltpu.CompilerParams(vmem_limit_bytes=4 << 20)


def split3(w):
    high = w.astype(BF16).astype(F32)
    mid = (w - high).astype(BF16).astype(F32)
    return high, mid, w - high - mid


def weights_kernel(head, reg, kernels, band, band_t, matrices, rows, arrived):
    tap_count, hidden_count, channels = reg.shape
    planes = band.shape[0]
    load = pltpu.make_async_copy(kernels, matrices, arrived)
    load.start()
    rows[...] = jnp.zeros_like(rows)
    for t in range(tap_count):
        row = head[0] * reg[t, 0:1, :].astype(F32)
        for r in range(1, hidden_count):
            row = row + head[r] * reg[t, r : r + 1, :].astype(F32)
        rows[t : t + 1, 0:channels] = row
    columns = rows[...].T
    lane = lax.broadcasted_iota(jnp.int32, (channels, BLK), 1)
    part = lane // planes
    score = lane % planes
    weights = []
    for t in range(tap_count):
        high, mid, low = split3(
            jnp.broadcast_to(columns[0:channels, t : t + 1], (channels, BLK))
        )
        weights.append(jnp.where(part < 2, high, jnp.where(part == 2, mid, low)))
    for d in range(planes):
        tile = jnp.zeros((channels, BLK), F32)
        for t in range(tap_count):
            tile = jnp.where(score == d - t + 1, weights[t], tile)
        band[d] = tile.astype(BF16)
    per_tile = BLK // channels
    for k in range(planes // per_tile):
        tile = band[k * per_tile : (k + 1) * per_tile].reshape(BLK, BLK)
        band_t[:, k * BLK : (k + 1) * BLK] = tile.astype(F32).T.astype(BF16)
    load.wait()


def stage_kernel(*refs):
    count = len(refs) // 2
    sems = refs[-1]
    copies = [
        pltpu.make_async_copy(refs[i], refs[count + i], sems.at[i]) for i in range(count)
    ]
    for copy in copies:
        copy.start()
    for copy in copies:
        copy.wait()


def table_kernel(mine, partner, out):
    planes = mine.shape[3]
    half = mine.shape[2] // 2

    def fill(start):
        for g, offsets in enumerate((mine, partner)):
            for j in range(V):
                for b in range(half):
                    row = offsets[0, j, start + b : start + b + 1, :]
                    out[g * V + j : g * V + j + 1, b * planes : (b + 1) * planes] = row

    pl.when(side() == 0)(lambda: fill(0))
    pl.when(side() == 1)(lambda: fill(half))


def side():
    return (lax.axis_index("frame") + lax.axis_index("tile")) % 2


def at_end():
    tile = lax.axis_index("tile")
    return jnp.where(side() == 0, tile == 0, tile == lax.axis_size("tile") - 1)


def halve_kernel(mine, partner, out):
    half = out.shape[1]

    def copy(start):
        for g, tile in enumerate((mine, partner)):
            for q in range(half):
                at = (start + q) * BLK
                out[g, q] = tile[0, :, at : at + BLK]

    pl.when(side() == 0)(lambda: copy(0))
    pl.when(side() == 1)(lambda: copy(half))


def rim_kernel(*refs):
    pieces, (outer, inner) = refs[:-2], refs[-2:]
    half = pieces[0].shape[1]
    left, right = slice(0, HB), slice(half - HB, half)

    def copy(out, part):
        for i, piece in enumerate(pieces):
            out[2 * i : 2 * i + 2] = piece[:, part]

    @pl.when(side() == 0)
    def _():
        copy(outer, left)
        copy(inner, right)

    @pl.when(side() == 1)
    def _():
        copy(outer, right)
        copy(inner, left)


class Work:
    def __init__(self, views, table, matrices, half, far):
        self.table, self.matrices = table, matrices
        self.half, self.slots = half, lax.axis_size("frame")
        self.planes = matrices.shape[0]
        self.span = half + 2 * HB
        self.me, self.side = lax.axis_index("frame"), side()
        blocks = half - HB if far else HB
        self.first = jnp.where((self.side == 0) == far, HB if far else half - HB, 0)
        self.columns = [(g, b) for g in range(2) for b in range(blocks)]
        self.slot_of = [[views[j, self.me ^ g] ^ self.me for j in range(V)] for g in range(2)]

    def lanes(self, k):
        return slice(k * BLK, (k + 1) * BLK)

    def rows_of(self, k, i, channels):
        start = (k * (V // 2) + i) * channels
        return slice(start, start + channels)

    def block_of(self, d, g, b, j):
        at = self.first + b
        return self.table[g * V + j, at * self.planes + d] + (at + HB)

    def pair_matrix(self, d):
        matrix = self.matrices[d]
        upper = jnp.concatenate([matrix, matrix], axis=1)
        return jnp.concatenate([upper, jnp.concatenate([matrix, -matrix], axis=1)], axis=0)

    def gather(self, src, base, pieces, outer, inner):
        half, span = self.half, self.span
        for r in range(self.slots):
            src[r * span + HB : r * span + HB + half] = pieces[r // 2][r % 2]

        def rims(near, far):
            for r in range(self.slots):
                if outer is not None:
                    src[r * span + near : r * span + near + HB] = outer[r]
                src[r * span + far : r * span + far + HB] = inner[r ^ 1]

        pl.when(self.side == 0)(lambda: rims(0, HB + half))
        pl.when(self.side == 1)(lambda: rims(HB + half, 0))
        if outer is not None:

            @pl.when(at_end())
            def _():
                near = jnp.where(self.side == 0, 0, HB + half)
                for r in range(self.slots):
                    for q in range(HB):
                        src[r * span + q + near] = jnp.zeros_like(src[0])

        for k, (g, b) in enumerate(self.columns):
            base[:, self.lanes(k)] = 2.0 * pieces[0][g, self.first + b].astype(F32)

    def forward(self, src, base, shifted, means, volume):
        pairs, share = V // 2, 1.0 / (V + 1)
        channels = base.shape[0]

        def plane(d, carry):
            picked = []
            for g, b in self.columns:
                for i in range(pairs):
                    tiles = [
                        src[self.slot_of[g][j] * self.span + self.block_of(d, g, b, j)]
                        for j in (2 * i, 2 * i + 1)
                    ]
                    picked.append(jnp.concatenate(tiles, axis=1))
            warped = jnp.dot(
                jnp.concatenate(picked, axis=0), self.pair_matrix(d), preferred_element_type=F32
            )
            for k in range(len(self.columns)):
                lanes = self.lanes(k)
                rows = [self.rows_of(k, i, channels) for i in range(pairs)]
                twice_first = base[:, lanes]
                plus = [warped[rows[i], 0:BLK] - twice_first for i in range(pairs)]
                minus = [warped[rows[i], BLK:] for i in range(pairs)]
                for i in range(pairs):
                    shifted[d, 2 * i, :, lanes] = plus[i]
                    shifted[d, 2 * i + 1, :, lanes] = minus[i]
                total = sum(plus[1:], plus[0])
                twice_mean = total * (2.0 * share)
                squares = sum(x * x for x in plus) + sum(x * x for x in minus)
                variance = (squares - total * twice_mean) * (0.5 * share)
                volume[d, :, lanes] = variance.astype(BF16)
                centred = total - (0.5 / share) * twice_mean
                means[d, :, lanes] = twice_mean + centred * (2.0 * share)
            return carry

        lax.fori_loop(0, self.planes, plane, 0, unroll=FORWARD)

    def depths(self, band, band_t, cots, volume, dvolume, depths, first):
        planes = self.planes
        channels = volume.shape[1]
        wide = len(self.columns) // 2 * BLK
        groups = [slice(g * wide, (g + 1) * wide) for g in range(2)]
        values = (
            lax.broadcasted_iota(jnp.int32, (planes, wide), 0).astype(F32) + 1.0
        ) / planes
        raws = []
        for lanes in groups:
            parts = jnp.dot(
                jnp.concatenate([band_t[0:planes], band_t[2 * planes :]], axis=0),
                volume[:, :, lanes].reshape(planes * channels, wide),
                preferred_element_type=F32,
            )
            raws.append(
                parts[0:planes]
                + (parts[planes : 2 * planes] + parts[2 * planes : 3 * planes])
            )
        stacks = []
        start = first * BLK
        start_cot = pl.multiple_of((self.side * self.half + self.first) * BLK, BLK)
        for g, raw in enumerate(raws):
            slope_in = cots[g][0:1, pl.ds(start_cot, wide)]
            tanh = jnp.tanh(raw)
            weights = jnp.exp(4.0 * tanh)
            norm = jnp.sum(weights, axis=0, keepdims=True)
            result = jnp.sum(weights * values, axis=0, keepdims=True) / norm
            depths[g][0:1, pl.ds(pl.multiple_of(start, BLK), wide)] = result
            slope = (slope_in / norm) * (values - result) * weights
            draw = slope * (4.0 * (1.0 - tanh * tanh))
            high = draw.astype(BF16)
            low = (draw - high.astype(F32)).astype(BF16)
            stacks.append(jnp.concatenate([high, low, high, high], axis=0))
        for lanes, stack in zip(groups, stacks):
            cotangent = jnp.dot(
                band[...].reshape(planes * channels, BLK), stack, preferred_element_type=F32
            )
            dvolume[:, :, lanes] = cotangent.astype(BF16).reshape(planes, channels, wide)

    def backward(self, shifted, means, dvolume, ref_grad, grads, sums):
        pairs = V // 2
        channels = ref_grad.shape[0]
        for grad in grads:
            grad[...] = jnp.zeros_like(grad)
        ref_grad[...] = jnp.zeros_like(ref_grad)

        def plane(d, carry):
            rows = []
            for k in range(len(self.columns)):
                lanes = self.lanes(k)
                dvar = dvolume[d, :, lanes].astype(F32)
                twice_mean = means[d, :, lanes]
                ref_grad[:, lanes] -= dvar * twice_mean
                for i in range(pairs):
                    plus = dvar * (shifted[d, 2 * i, :, lanes] - twice_mean)
                    minus = dvar * shifted[d, 2 * i + 1, :, lanes]
                    rows += [(plus + minus).astype(BF16), (plus - minus).astype(BF16)]
            dpicked = lax.dot_general(
                jnp.concatenate(rows, axis=0), self.matrices[d],
                (((1,), (1,)), ((), ())), preferred_element_type=F32,
            )
            for k, (g, b) in enumerate(self.columns):
                for j in range(V):
                    start = (k * V + j) * channels
                    grads[g * V + j][self.block_of(d, g, b, j)] += dpicked[start : start + channels]
            return carry

        lax.fori_loop(0, self.planes, plane, 0, unroll=BACKWARD)
        for k, (g, b) in enumerate(self.columns):
            sums[g * self.span + HB + self.first + b] += ref_grad[:, self.lanes(k)]
        for g in range(2):
            for j in range(V):
                sums[pl.ds(self.slot_of[g][j] * self.span, self.span)] += grads[g * V + j][...]

    def give(self, sums, out, outer):
        end = HB + self.half

        def copy(start):
            for r in range(self.slots):
                at = r * self.span + start
                out[r] = (sums[at : at + HB] * (1.0 / (V + 1))).astype(BF16)

        pl.when(self.side == 0)(lambda: copy(0 if outer else end))
        pl.when(self.side == 1)(lambda: copy(end if outer else 0))


def forward_kernel(views, table, inner, matrices, band, band_t, cot, cot_partner, *refs):
    pieces, (shifted, means, dvolume, depth, depth_partner, src, base) = refs[:-7], refs[-7:]
    work = Work(views, table, matrices, pieces[0].shape[1], True)
    work.gather(src, base, pieces, None, inner)
    work.forward(src, base, shifted, means, dvolume)
    work.depths(
        band, band_t, (cot, cot_partner), dvolume, dvolume, (depth, depth_partner), 0
    )


def depth_kernel(
    views, table, outer, inner, matrices, band, band_t, cot, cot_partner, far_depth,
    far_depth_partner, *refs,
):
    (
        depth, depth_partner, grad_outer, sums,
        src, base, shifted, means, volume, ref_grad,
    ) = refs[-10 - 2 * V : -2 * V]
    pieces, grads = refs[: -10 - 2 * V], refs[-2 * V :]
    half = pieces[0].shape[1]
    near = Work(views, table, matrices, half, False)
    near.gather(src, base, pieces, outer, inner)
    near.forward(src, base, shifted, means, volume)
    near.depths(
        band, band_t, (cot, cot_partner), volume, volume, (depth, depth_partner), near.first
    )
    far_at = pl.multiple_of(jnp.where(near.side == 0, HB, 0) * BLK, BLK)
    far_wide = far_depth.shape[1]
    depth[0:1, pl.ds(far_at, far_wide)] = far_depth[...]
    depth_partner[0:1, pl.ds(far_at, far_wide)] = far_depth_partner[...]
    sums[...] = jnp.zeros_like(sums)
    near.backward(shifted, means, volume, ref_grad, grads, sums)
    near.give(sums, grad_outer, True)


def backward_kernel(
    views, table, matrices, shifted, means, dvolume, sums_in,
    core_grad, grad_inner, sums, ref_grad, *grads,
):
    half = core_grad.shape[1]
    work = Work(views, table, matrices, half, True)
    sums[...] = sums_in[...]
    work.backward(shifted, means, dvolume, ref_grad, grads, sums)
    for r in range(work.slots):
        at = r * work.span + HB
        core_grad[r] = sums[at : at + half] * (1.0 / (V + 1))
    work.give(sums, grad_inner, False)


def merge_kernel(core, outer, inner, own, *sent):
    slots, half = core.shape[:2]

    def merge(near, far, beyond):
        for r in range(slots):
            out = own if r < 2 else sent[r // 2 - 1]
            for q in range(half):
                tile = core[r, q]
                if beyond and near <= q < near + HB:
                    tile = tile + outer[r, q - near].astype(F32)
                if far <= q < far + HB:
                    tile = tile + inner[r ^ 1, q - far].astype(F32)
                out[r % 2, q] = tile.astype(out.dtype)

    for i, ends in enumerate(((0, half - HB), (half - HB, 0))):
        here = side() == i
        pl.when(here & at_end())(lambda ends=ends: merge(*ends, False))
        pl.when(here & jnp.logical_not(at_end()))(lambda ends=ends: merge(*ends, True))


def sum_kernel(own, *refs):
    received, (mine, partner) = refs[:-2], refs[-2:]
    for g, out in enumerate((mine, partner)):
        total = own[g]
        for piece in received:
            total = total + piece[g].astype(F32)
        out[...] = total.astype(out.dtype)


def join_kernel(mine, partner, depth_mine, depth_partner, grad, depth):
    half = mine.shape[0]

    def join(at, tile, part):
        for q in range(half):
            grad[0, :, (at + q) * BLK : (at + q + 1) * BLK] = tile[q].astype(F32)
        depth[:, at * BLK : (at + half) * BLK] = part[...]

    @pl.when(side() == 0)
    def _():
        join(0, mine, depth_mine)
        join(half, partner, depth_partner)

    @pl.when(side() == 1)
    def _():
        join(0, partner, depth_partner)
        join(half, mine, depth_mine)


def exchange(x, distance):
    count = lax.axis_size("frame")
    return lax.ppermute(x, "frame", [(i, i ^ distance) for i in range(count)])


def swap_outer(x):
    count, tiles = lax.axis_size("frame"), lax.axis_size("tile")
    pairs = [
        (f * tiles + t, f * tiles + t + 1)
        for f in range(count)
        for t in range(tiles - 1)
        if (f + t) % 2 == 1
    ]
    ends = [(f, 0) for f in range(count) if f % 2 == 0]
    ends += [(f, tiles - 1) for f in range(count) if (f + tiles - 1) % 2 == 1]
    if count >= 4:
        pairs += [(f * tiles + t, (f ^ 2) * tiles + t) for f, t in ends if f & 2 == 0]
    return lax.ppermute(x, ("frame", "tile"), pairs + [(b, a) for a, b in pairs])


def small_call(kernel, ins, outs, scratch=()):
    return pl.pallas_call(
        kernel, out_shape=outs, in_specs=ins, out_specs=jax.tree.map(lambda _: VMEM, outs),
        scratch_shapes=scratch, compiler_params=SMALL,
    )


def per_device(features, views, offsets, kernels, reg_weight, head_weight, depth_cot):
    local_frames, channels, pixels = features.shape
    frames = lax.axis_size("frame")
    half = pixels // BLK // 2
    planes = kernels.shape[0]
    assert local_frames == 1 and frames & (frames - 1) == 0
    assert pixels == 2 * half * BLK and half >= HB
    shape = jax.ShapeDtypeStruct
    rim_shape = shape((frames, HB, channels, BLK), BF16)
    pair_shape = shape((2, half, channels, BLK), BF16)
    half_shape = shape((half, channels, BLK), F32)
    views = views.T
    offsets = jnp.swapaxes(offsets, 2, 3)

    features_partner = exchange(features, 1)
    arguments = (features, views, reg_weight, head_weight, offsets, depth_cot)
    staged, views, reg_weight, head_weight, offsets_mine, cot_mine = pl.pallas_call(
        stage_kernel,
        out_shape=tuple(shape(x.shape, x.dtype) for x in arguments),
        in_specs=[pl.BlockSpec(memory_space=pltpu.HBM)] * len(arguments),
        out_specs=(VMEM,) * len(arguments),
        scratch_shapes=[pltpu.SemaphoreType.DMA((len(arguments),))],
        compiler_params=SMALL,
        name="stage_arguments",
    )(*(pltpu.with_memory_space_constraint(x, pltpu.HBM) for x in arguments))
    prepare = small_call(
        weights_kernel, [SMEM, VMEM, pl.BlockSpec(memory_space=pltpu.HBM)],
        (
            shape((planes, channels, BLK), BF16), shape((BLK, planes * channels), BF16),
            shape(kernels.shape, BF16),
        ),
        [pltpu.VMEM((BLK, BLK), F32), pltpu.SemaphoreType.DMA(())],
    )
    band, band_t, matrices = prepare(head_weight, reg_weight, pltpu.with_memory_space_constraint(kernels, pltpu.HBM))

    offsets_partner = exchange(offsets, 1)
    table = small_call(
        table_kernel, [VMEM] * 2, shape((2 * V, half * planes), jnp.int32)
    )(offsets_mine, offsets_partner)
    cot_partner = exchange(depth_cot, 1)
    pieces = [small_call(halve_kernel, [VMEM] * 2, pair_shape)(staged, features_partner)]
    for r in range(2, frames, 2):
        pieces.append(exchange(pieces[0], r))
    outer, inner = small_call(rim_kernel, [VMEM] * (frames // 2), (rim_shape, rim_shape))(*pieces)
    inner = exchange(inner, 1)
    outer = swap_outer(outer)

    span = half + 2 * HB
    assert V % 2 == 0 and planes % FORWARD == 0
    near_pixels, far_pixels = 2 * HB * BLK, 2 * (half - HB) * BLK
    depth_half = shape((1, half * BLK), F32)
    sums_shape = shape((frames * span, channels, BLK), F32)
    sources = pltpu.VMEM((frames * span, channels, BLK), BF16)
    accumulators = [pltpu.VMEM((span, channels, BLK), F32)] * (2 * V)

    def big_call(kernel, smem, vmem, outs, scratch, limit, part):
        return pl.pallas_call(
            kernel, out_shape=outs, in_specs=[SMEM] * smem + [VMEM] * vmem,
            out_specs=jax.tree.map(lambda _: VMEM, outs), scratch_shapes=scratch,
            compiler_params=pltpu.CompilerParams(vmem_limit_bytes=limit << 20),
            cost_estimate=pl.CostEstimate(
                flops=int(part * planes * V * channels * pixels * BLK),
                bytes_accessed=4 << 20, transcendentals=2 * planes * pixels,
            ),
        )

    far_half = shape((1, far_pixels // 2), F32)
    shifted, means, dvolume, *far_depths = big_call(
        forward_kernel, 2, 6 + frames // 2,
        (
            shape((planes, V, channels, far_pixels), F32),
            shape((planes, channels, far_pixels), F32),
            shape((planes, channels, far_pixels), BF16),
            far_half, far_half,
        ),
        [sources, pltpu.VMEM((channels, far_pixels), F32)], 4, 1,
    )(views, table, inner, matrices, band, band_t, cot_mine, cot_partner, *pieces)
    depth, depth_partner, outer, sums = big_call(
        depth_kernel, 2, 9 + frames // 2,
        (depth_half, depth_half, rim_shape, sums_shape),
        [
            sources,
            pltpu.VMEM((channels, near_pixels), F32),
            pltpu.VMEM((planes, V, channels, near_pixels), F32),
            pltpu.VMEM((planes, channels, near_pixels), F32),
            pltpu.VMEM((planes, channels, near_pixels), BF16),
            pltpu.VMEM((channels, near_pixels), F32),
        ]
        + accumulators, 20, 2,
    )(
        views, table, outer, inner, matrices, band, band_t, cot_mine, cot_partner,
        *far_depths, *pieces,
    )
    outer = swap_outer(outer)
    core_grad, inner = big_call(
        backward_kernel, 2, 5,
        (shape((frames, half, channels, BLK), F32), rim_shape),
        [
            pltpu.VMEM(sums_shape.shape, F32), pltpu.VMEM((channels, far_pixels), F32),
        ]
        + accumulators, 6, 1,
    )(views, table, matrices, shifted, means, dvolume, sums)
    inner = exchange(inner, 1)
    depth_partner = exchange(depth_partner, 1)
    own, *sent = small_call(
        merge_kernel, [VMEM] * 3,
        (shape(pair_shape.shape, F32),) + (pair_shape,) * (frames // 2 - 1),
    )(core_grad, outer, inner)
    received = []
    for r, piece in zip(range(2, frames, 2), sent):
        received.append(exchange(piece, r))
    mine, partner = small_call(
        sum_kernel, [VMEM] * (frames // 2), (half_shape, shape(half_shape.shape, BF16))
    )(own, *received)
    grad, depth = small_call(
        join_kernel, [VMEM] * 4,
        (shape(features.shape, F32), shape(depth_cot.shape, F32)),
    )(mine, exchange(partner, 1), depth, depth_partner)
    return depth, grad


def solution(mesh):
    return jax.shard_map(
        per_device,
        mesh=mesh,
        in_specs=(
            P("frame", None, "tile"),
            P(),
            P("frame", None, None, "tile"),
            P(),
            P(),
            P(),
            P("frame", "tile"),
        ),
        out_specs=(P("frame", "tile"), P("frame", None, "tile")),
        check_vma=False,
    )
```
